32 devices in a mesh: grp: 2 (over x), sp: 16 (over z, y, core).
Axes of the slice: x: 2, y: 2, z: 4, core: 2. Of those that a mesh axis runs over, the one named last changes fastest.
Arguments:
- latents: bfloat16 [10240, 64], P(('grp', 'sp')), parts along dimension 0, may hold values from -9 to 9
- row_cell: int32 [10240], P(('grp', 'sp')), parts along dimension 0, may hold values from 0 to 5119, as said below
- w_in: bfloat16 [3, 3, 3, 16, 384], replicated, may hold values from -1 to 1
- b_in: float32 [384], replicated, may hold values from -3 to 3
- gain: float32 [384], replicated, may hold values from 0.1 to 1.9
- w_mid: bfloat16 [3, 3, 3, 384, 384], replicated, may hold values from -0.0625 to 0.0625
- b_mid: float32 [384], replicated, may hold values from -3 to 3
Outputs:
- decoded: bfloat16 [32, 2, 4, 160, 384], P(('grp', 'sp')), parts along dimension 0
The draws below stay inside these ranges and needn't reach their ends.
There are 2 independent parts, one for each index of `grp`. The reference program is written for one: setup_inputs(seed, part) draws one part's arguments, and reference() takes and returns one part's arrays. A program takes and returns all parts, laid end to end along the dimension named above; an argument that names none is the same for every part. Nothing has to cross between parts.
Inputs may be any that keep to these rules, and one draw needn't show every extreme that they name: `row_cell`: every token position appears exactly once. The tile of token (t, i, j) is (t // 2) * 8 + (2 i) // 4. Among the tokens of one device, every tile has 20 tokens, except one tile with 40 and one with none; each tile gets 2 * 20 tokens from exactly one device. Order within a device is arbitrary.
All inputs are finite; a program needn't handle non-finite values.
Results may differ from the reference program's by a relative error of at most 0.0051.
Values may be sent and summed in bfloat16 or wider, within the bound.
No kernel may reach another device: no remote copies, remote signals or barrier semaphores. Data moves between devices by JAX's collectives and lax.ppermute only.
A program may use at most 128 MiB of HBM per device.

```python
import math
import jax
import jax.numpy as jnp
from jax import lax

C_LAT = 16
C_MID = 384
W = 160
TB = 2
HBANDS = 8
HB = 4
TBLOCKS = 2
TILES = 16
FRAMES = 4
HEIGHT = 32
TOKS = 320
TOKENS = 5120
PAIR = 20


def draw_latents(key, part):
    base = jnp.clip(jax.random.normal(jax.random.fold_in(key, 11), (TOKENS, 4 * C_LAT), jnp.float32), -6.0, 6.0)
    return base.astype(jnp.bfloat16)


def draw_w_in(key, part):
    columns = jnp.exp(jax.random.uniform(jax.random.fold_in(key, 21), (C_MID,), jnp.float32, math.log(0.3), math.log(3.0)))
    entries = jnp.clip(jax.random.normal(jax.random.fold_in(key, 22), (3, 3, 3, C_LAT, C_MID), jnp.float32), -4.0, 4.0)
    return (entries * columns / math.sqrt(27.0 * C_LAT)).astype(jnp.bfloat16)


def draw_row_cell(key, part):
    count = TILES
    keys = jax.random.split(jax.random.fold_in(key, 5), 3)
    favoured = jax.random.permutation(keys[0], count).astype(jnp.int32)
    skipped = jnp.roll(favoured, 1)
    owners = jnp.arange(count, dtype=jnp.int32)
    pair_counts = PAIR + PAIR * ((favoured[:, None] == owners[None, :]).astype(jnp.int32) - (skipped[:, None] == owners[None, :]).astype(jnp.int32))
    upto = jnp.cumsum(pair_counts, axis=0)
    starts = upto - pair_counts
    src_offsets = jnp.cumsum(pair_counts, axis=1) - pair_counts
    within = jnp.arange(TOKS, dtype=jnp.int32)
    source = jnp.sum((upto[:, :, None] <= within[None, None, :]).astype(jnp.int32), axis=0)
    start_of = jnp.take_along_axis(starts.T, source, axis=1)
    offset_of = jnp.take_along_axis(src_offsets.T, source, axis=1)
    place = offset_of + within[None, :] - start_of
    tile_orders = jax.vmap(lambda sub: jax.random.permutation(sub, TOKS))(jax.random.split(keys[1], count)).astype(jnp.int32)
    shuffles = jax.vmap(lambda sub: jax.random.permutation(sub, TOKS))(jax.random.split(keys[2], count)).astype(jnp.int32)
    final_place = source * TOKS + shuffles[source, place]
    half_rows = HB // 2
    half_width = W // 2
    frame_in = tile_orders // (half_rows * half_width)
    row_in = tile_orders // half_width % half_rows
    col_in = tile_orders % half_width
    tile_time = (owners // HBANDS)[:, None]
    tile_band = (owners % HBANDS)[:, None]
    cell = ((tile_time * TB + frame_in) * (HEIGHT // 2) + tile_band * half_rows + row_in) * half_width + col_in
    return jnp.zeros((TOKENS,), jnp.int32).at[final_place.reshape(-1)].set(cell.reshape(-1).astype(jnp.int32))


def bell_draw(rng, extent, width, reach, kind=jnp.bfloat16):
    return jnp.clip(width * jax.random.normal(rng, extent, jnp.float32), -reach, reach).astype(kind)


def setup_inputs(seed: int = 0, part: int = 0) -> dict:
    splits = jax.random.split(jax.random.key(seed), 8)
    own_keys = jax.random.split(jax.random.fold_in(splits[7], part), 8)
    return {
        "latents": draw_latents(jax.random.fold_in(jax.random.fold_in(splits[7], part), 71), part),
        "row_cell": draw_row_cell(jax.random.fold_in(jax.random.fold_in(splits[7], part), 71), part),
        "w_in": draw_w_in(jax.random.fold_in(splits[7], 71), part),
        "b_in": bell_draw(splits[3], (C_MID,), 0.5, 3.0, jnp.float32),
        "gain": jnp.clip(1.0 + 0.18 * jax.random.normal(splits[4], (C_MID,), jnp.float32), 0.1, 1.9),
        "w_mid": bell_draw(splits[5], (3, 3, 3, C_MID, C_MID), (27 * C_MID) ** -0.5, 0.0625),
        "b_mid": bell_draw(splits[6], (C_MID,), 0.5, 3.0, jnp.float32),
    }


def causal_conv(extended, weight):
    frames_out = extended.shape[0] - 2
    rows_out = extended.shape[1] - 2
    tile_width = extended.shape[2]
    channels = extended.shape[3]
    outputs = weight.shape[4]
    padded = jnp.pad(extended, ((0, 0), (0, 0), (1, 1), (0, 0)))
    widened = jnp.concatenate([padded[:, :, offset:offset + tile_width] for offset in range(3)], axis=3)
    accumulated = jnp.zeros((frames_out, rows_out, tile_width, outputs), jnp.float32)
    for tap_time in range(3):
        for tap_row in range(3):
            window = widened[tap_time:tap_time + frames_out, tap_row:tap_row + rows_out]
            kernel = weight[tap_time, tap_row].reshape(3 * channels, outputs)
            accumulated = accumulated + jnp.einsum('thwc,cd->thwd', window.astype(jnp.float32), kernel.astype(jnp.float32))
    return accumulated

def rms_silu(hidden, gain):
    values = hidden.astype(jnp.float32)
    inverse_rms = lax.rsqrt(lax.optimization_barrier(jnp.mean(values * values, axis=-1, keepdims=True)) + 1e-06)
    return jax.nn.silu(values * inverse_rms * gain).astype(jnp.bfloat16)

def reference(latents, row_cell, w_in, b_in, gain, w_mid, b_mid):
    latent_grid = jnp.zeros((TOKENS, 4 * C_LAT), jnp.bfloat16).at[row_cell].set(latents)
    latent_grid = latent_grid.reshape(FRAMES, HEIGHT // 2, W // 2, 2, 2, C_LAT)
    latent_grid = latent_grid.transpose(0, 1, 3, 2, 4, 5).reshape(FRAMES, HEIGHT, W, C_LAT)
    padded_latents = jnp.pad(latent_grid, ((2, 0), (1, 1), (0, 0), (0, 0)))
    hidden = (causal_conv(padded_latents, w_in) + b_in).astype(jnp.bfloat16)
    activated = rms_silu(hidden, gain)
    padded_active = jnp.pad(activated, ((2, 0), (1, 1), (0, 0), (0, 0)))
    mixed = causal_conv(padded_active, w_mid) + b_mid + hidden.astype(jnp.float32)
    decoded = mixed.astype(jnp.bfloat16).reshape(TBLOCKS, TB, HBANDS, HB, W, C_MID)
    decoded = decoded.transpose(0, 2, 1, 3, 4, 5).reshape(TILES, TB, HB, W, C_MID)
    return jnp.roll(decoded, -(2 * HBANDS + HBANDS // 2), axis=0)
```

```python
import functools

import jax
import jax.numpy as jnp
from jax import lax
from jax.experimental import pallas as pl
from jax.experimental.pallas import tpu as pltpu
from jax.sharding import PartitionSpec as P

C_LAT = 16
W = 160
TB = 2
HBANDS = 8
HB = 4
OFFSET = 2 * HBANDS + HBANDS // 2
HALF_ROWS = HB // 2
HALF_W = W // 2
TILE_TOKENS = TB * HALF_ROWS * HALF_W
PATCH = 4 * C_LAT
F32 = jnp.float32
BF16 = jnp.bfloat16
VMEM = pl.BlockSpec(memory_space=pltpu.VMEM)
ANY = pl.BlockSpec(memory_space=pl.ANY)


def place_code(index):
    return ((index & 127) + 128) << (index >> 7)


def pack_kernel(devices, rows, half, cells_ref, latents_ref, out_ref):
    tokens = latents_ref.shape[0]
    cells = cells_ref[...]
    column = lax.rem(cells, HALF_W)
    token_row = lax.rem(lax.div(cells, HALF_W), HALF_ROWS * HBANDS)
    frame = lax.div(cells, HALF_W * HALF_ROWS * HBANDS)
    block = lax.div(frame, TB)
    band = lax.div(token_row, HALF_ROWS)
    side = lax.rem(token_row, HALF_ROWS)
    local = (lax.rem(frame, TB) * HALF_ROWS + side) * HALF_W + column
    code = place_code((lax.rem(block, 3) * 3 + lax.rem(band, 3)) * TILE_TOKENS + local)
    code = code.astype(F32)

    device = lax.broadcasted_iota(jnp.int32, (devices, tokens), 0)
    tile = lax.rem(device + OFFSET, devices)
    to_band = lax.rem(tile, HBANDS)
    age = lax.div(tile, HBANDS) - block
    near = (
        (band == to_band)
        | ((band == to_band - 1) & (side == HALF_ROWS - 1))
        | ((band == to_band + 1) & (side == 0))
    )
    hits = jnp.where((age >= 0) & (age < 3) & near, 1.0, 0.0)
    before = lax.broadcasted_iota(jnp.int32, (tokens, tokens), 0) < lax.broadcasted_iota(
        jnp.int32, (tokens, tokens), 1
    )
    before = jnp.where(before, 1.0, 0.0).astype(BF16)
    rank = jnp.dot(hits.astype(BF16), before, preferred_element_type=F32)
    rank = jnp.where(hits > 0.5, rank, -1.0)

    slot = lax.broadcasted_iota(jnp.int32, (rows, tokens), 0).astype(F32)
    low_slot = jnp.where(slot < half, slot, -7.0)
    high_slot = jnp.where(slot < half, slot + half, -7.0)
    low = jnp.concatenate(
        [jnp.where(rank[d : d + 1] == low_slot, 1.0, 0.0).astype(BF16) for d in range(devices)], 0
    )
    high = jnp.concatenate(
        [jnp.where(rank[d : d + 1] == high_slot, 1.0, 0.0).astype(BF16) for d in range(devices)], 0
    )
    latents = latents_ref[...]
    blank = jnp.zeros_like(latents)
    codes = jnp.transpose(jnp.broadcast_to(code, (128, tokens))).astype(BF16)
    low_out = jnp.dot(
        low, jnp.concatenate([latents, blank, codes], 1), preferred_element_type=F32
    )
    high_out = jnp.dot(
        high, jnp.concatenate([blank, latents, codes], 1), preferred_element_type=F32
    )
    row = lax.broadcasted_iota(jnp.int32, (rows, 128), 0)
    diagonal = row == lax.broadcasted_iota(jnp.int32, (rows, 128), 1)
    for d in range(devices):
        part = slice(d * rows, (d + 1) * rows)
        low_codes = jnp.sum(jnp.where(diagonal, low_out[part, 128:], 0.0), 0, keepdims=True)
        high_codes = jnp.sum(jnp.where(diagonal, high_out[part, 128:], 0.0), 0, keepdims=True)
        body = low_out[part, :128] + high_out[part, :128]
        body = jnp.where(row == rows - 2, low_codes, body)
        body = jnp.where(row == rows - 1, high_codes, body)
        out_ref[part, :] = body.astype(BF16)


def main_kernel(
    devices,
    blocks,
    arrived_ref,
    w_in_ref,
    b_in_ref,
    gain_ref,
    w_mid_hbm,
    b_mid_ref,
    out_ref,
    w_mid_ref,
    edge_ref,
    active_ref,
    hidden_ref,
    mix_ref,
    w_sem,
):
    weights_copy = pltpu.make_async_copy(w_mid_hbm, w_mid_ref, w_sem)
    weights_copy.start()
    total = arrived_ref.shape[0]
    rows = total // devices
    c_mid = gain_ref.shape[1]
    tile = lax.rem(lax.axis_index("sp") + OFFSET, devices)
    band = lax.rem(tile, HBANDS)
    time_block = lax.div(tile, HBANDS)

    arrived = arrived_ref[...]
    low_codes = jnp.concatenate(
        [arrived[(s + 1) * rows - 2 : (s + 1) * rows - 1, :rows] for s in range(devices)], 1
    ).astype(F32)
    high_codes = jnp.concatenate(
        [arrived[(s + 1) * rows - 1 : (s + 1) * rows, :rows] for s in range(devices)], 1
    ).astype(F32)
    k = lax.broadcasted_iota(jnp.int32, (128, 256), 0)
    lane = lax.broadcasted_iota(jnp.int32, (128, 256), 1)
    within = lane & 63
    swap = ((lane >> 6) ^ (lane >> 7)) & 1
    source = swap * (2 * C_LAT) + jnp.where(
        within < C_LAT,
        within + C_LAT,
        jnp.where(within < 3 * C_LAT, within - C_LAT, within - 3 * C_LAT),
    )
    low_spread = jnp.where(k == source, 1.0, 0.0).astype(BF16)
    high_spread = jnp.where(k == source + PATCH, 1.0, 0.0).astype(BF16)
    low_tokens = jnp.dot(arrived, low_spread, preferred_element_type=F32).astype(BF16)
    high_tokens = jnp.dot(arrived, high_spread, preferred_element_type=F32).astype(BF16)

    column = lax.broadcasted_iota(jnp.int32, (HALF_W, 1), 0)
    lanes = lax.broadcasted_iota(jnp.int32, (1, 1, 256), 2) & 63
    from_left, from_right = lanes < C_LAT, lanes >= 3 * C_LAT
    first = lax.broadcasted_iota(jnp.int32, (1, 1, 128), 2) < PATCH
    token_rows = HALF_ROWS + 2
    for f in range(TB * blocks):
        low_pick, high_pick = [], []
        frame = (time_block - (blocks - 1)) * TB + f
        for i in range(token_rows):
            token_row = band * HALF_ROWS - 1 + i
            valid = (frame >= 0) & (token_row >= 0) & (token_row < HALF_ROWS * HBANDS)
            frame_in = lax.max(frame, 0)
            row_in = lax.max(token_row, 0)
            base = (
                lax.rem(lax.div(frame_in, TB), 3) * 3 + lax.rem(lax.div(row_in, HALF_ROWS), 3)
            ) * TILE_TOKENS + (
                lax.rem(frame_in, TB) * HALF_ROWS + lax.rem(row_in, HALF_ROWS)
            ) * HALF_W
            code = jnp.where(valid, place_code(base + column), -1).astype(F32)
            low_pick.append(jnp.where(low_codes == code, 1.0, 0.0).astype(BF16))
            high_pick.append(jnp.where(high_codes == code, 1.0, 0.0).astype(BF16))
        placed = jnp.dot(
            jnp.concatenate(low_pick, 0), low_tokens, preferred_element_type=F32
        ) + jnp.dot(jnp.concatenate(high_pick, 0), high_tokens, preferred_element_type=F32)
        placed = placed.reshape(token_rows, HALF_W, 256)
        gap = jnp.zeros((token_rows, 1, 256), F32)
        left = jnp.concatenate([gap, placed[:, :-1]], 1)
        right = jnp.concatenate([placed[:, 1:], gap], 1)
        placed = jnp.where(from_left, left, jnp.where(from_right, right, placed))
        even_rows, odd_rows = placed[:, :, :128], placed[:, :, 128:]
        below = jnp.concatenate([odd_rows[1:], jnp.zeros((1, HALF_W, 128), F32)], 0)
        odd_rows = jnp.where(first, odd_rows, below)
        for i in range(token_rows):
            start = 2 * i * HALF_W
            edge_ref[f, start : start + HALF_W, :] = even_rows[i].astype(BF16)
            edge_ref[f, start + HALF_W : start + 2 * HALF_W, :] = odd_rows[i].astype(BF16)

    wide = (HB + 2) * HALF_W
    index = lax.broadcasted_iota(jnp.int32, (wide, 1), 0)
    global_row = band * HB - 1 + lax.div(index, HALF_W)
    inside = (global_row >= 0) & (global_row < HB * HBANDS)
    bias = b_in_ref[...]
    gain = gain_ref[...]
    for a in range(TB + 2):
        windows, kernels = [], []
        for tap in range(3):
            f = TB * (blocks - 1) - 4 + a + tap
            if f < 0:
                continue
            windows += [
                edge_ref[f, 0:wide, :],
                edge_ref[f, 2 * HALF_W : 2 * HALF_W + wide, :],
            ]
            kernels.append(w_in_ref[tap])
        sums = jnp.dot(
            jnp.concatenate(windows, 1), jnp.concatenate(kernels, 0), preferred_element_type=F32
        )
        keep = inside & (time_block * TB - 2 + a >= 0)
        for p in range(2):
            part = slice(p * c_mid, (p + 1) * c_mid)
            hidden = (sums[:, part] + bias).astype(BF16)
            if a >= 2:
                hidden_ref[a - 2, :, part] = hidden[HALF_W : HALF_W + HB * HALF_W]
            values = hidden.astype(F32)
            mean = jnp.sum(values * values, 1, keepdims=True) * (1.0 / c_mid)
            inverse = jnp.where(keep, lax.rsqrt(mean + 1e-06), 0.0)
            scaled = values * inverse * gain
            halved = scaled * 0.5
            active_ref[a, :, part] = (halved + halved * jnp.tanh(halved)).astype(BF16)

    weights_copy.wait()
    tall = HB * HALF_W
    for o in range(TB):
        windows, kernels = [], []
        evens, odds, rights, lefts = [], [], [], []
        for tap_time in range(3):
            for tap_row in range(3):
                start = tap_row * HALF_W
                windows.append(active_ref[o + tap_time, start : start + tall, :])
                w0, w1, w2 = (w_mid_ref[tap_time, tap_row, t] for t in range(3))
                kernels.append(jnp.concatenate([w1, w0], 1))
                kernels.append(jnp.concatenate([w2, w1], 1))
                evens.append(active_ref[o + tap_time, start : start + tall, :c_mid])
                odds.append(active_ref[o + tap_time, start : start + tall, c_mid:])
                rights.append(w2)
                lefts.append(w0)
        sums = jnp.dot(
            jnp.concatenate(windows, 1), jnp.concatenate(kernels, 0), preferred_element_type=F32
        )
        from_even = jnp.dot(
            jnp.concatenate(evens, 1), jnp.concatenate(rights, 0), preferred_element_type=F32
        ).reshape(HB, HALF_W, c_mid)
        from_odd = jnp.dot(
            jnp.concatenate(odds, 1), jnp.concatenate(lefts, 0), preferred_element_type=F32
        ).reshape(HB, HALF_W, c_mid)
        gap = jnp.zeros((HB, 1, c_mid), F32)
        to_odd = jnp.concatenate([from_even[:, 1:], gap], 1).reshape(tall, c_mid)
        to_even = jnp.concatenate([gap, from_odd[:, :-1]], 1).reshape(tall, c_mid)
        hidden = hidden_ref[o].astype(F32)
        bias_mid = b_mid_ref[...]
        even_out = sums[:, :c_mid] + to_even + bias_mid + hidden[:, :c_mid]
        odd_out = sums[:, c_mid:] + to_odd + bias_mid + hidden[:, c_mid:]
        for g in range(c_mid // 128):
            part = slice(g * 128, (g + 1) * 128)
            mix_ref[g, pl.ds(0, tall, stride=2), :] = even_out[:, part]
            mix_ref[g, pl.ds(1, tall, stride=2), :] = odd_out[:, part]
            out_ref[o * 2 * tall : (o + 1) * 2 * tall, part] = mix_ref[g].astype(BF16)


def input_kernel(w_in):
    c_mid = w_in.shape[-1]
    gap = jnp.zeros((3, 3, 1) + w_in.shape[3:], w_in.dtype)
    even = jnp.concatenate([w_in, gap], 2)
    odd = jnp.concatenate([gap, w_in], 2)
    both = jnp.concatenate([even, odd], -1).reshape(3, 3 * PATCH, 2 * c_mid)
    return jnp.pad(both, ((0, 0), (0, PATCH), (0, 0)))


def shards(latents, row_cell, w_in, b_in, gain, w_mid, b_mid):
    devices = lax.axis_size("sp")
    tokens = latents.shape[0]
    c_mid = gain.shape[0]
    blocks = min(3, devices // HBANDS)
    pair = tokens // devices
    slots = pair * 3 * blocks + pair
    half = -(-slots // 2)
    rows = -(-(half + 2) // 8) * 8
    outgoing = pl.pallas_call(
        functools.partial(pack_kernel, devices, rows, half),
        out_shape=jax.ShapeDtypeStruct((devices * rows, 128), BF16),
        in_specs=[VMEM, VMEM],
        out_specs=VMEM,
        name="pack",
    )(row_cell.reshape(1, tokens), latents)
    arrived = lax.all_to_all(
        outgoing.reshape(devices, rows, 128), "sp", split_axis=0, concat_axis=0, tiled=True
    )
    decoded = pl.pallas_call(
        functools.partial(main_kernel, devices, blocks),
        out_shape=jax.ShapeDtypeStruct((TB * HB * W, c_mid), BF16),
        in_specs=[VMEM, VMEM, VMEM, VMEM, ANY, VMEM],
        out_specs=VMEM,
        scratch_shapes=[
            pltpu.VMEM(w_mid.shape, BF16),
            pltpu.VMEM((TB * blocks, 2 * (HALF_ROWS + 2) * HALF_W, 128), BF16),
            pltpu.VMEM((TB + 2, (HB + 2) * HALF_W, 2 * c_mid), BF16),
            pltpu.VMEM((TB, HB * HALF_W, 2 * c_mid), BF16),
            pltpu.VMEM((c_mid // 128, HB * W, 128), F32),
            pltpu.SemaphoreType.DMA,
        ],
        compiler_params=pltpu.CompilerParams(vmem_limit_bytes=56 * 1024 * 1024),
        name="block",
    )(
        arrived.reshape(devices * rows, 128),
        input_kernel(w_in),
        b_in.reshape(1, c_mid),
        gain.reshape(1, c_mid),
        w_mid,
        b_mid.reshape(1, c_mid),
    )
    return decoded.reshape(1, TB, HB, W, c_mid)


def solution(mesh):
    return jax.shard_map(
        shards,
        mesh=mesh,
        in_specs=(P(("grp", "sp"), None), P(("grp", "sp")), P(), P(), P(), P(), P()),
        out_specs=P(("grp", "sp"), None, None, None, None),
        check_vma=False,
    )
```

```python
import functools

import jax
import jax.numpy as jnp
from jax import lax
from jax.experimental import pallas as pl
from jax.experimental.pallas import tpu as pltpu
from jax.sharding import PartitionSpec as P

C_LAT = 16
W = 160
TB = 2
HBANDS = 8
HB = 4
OFFSET = 2 * HBANDS + HBANDS // 2
HALF_ROWS = HB // 2
HALF_W = W // 2
TILE_TOKENS = TB * HALF_ROWS * HALF_W
PATCH = 4 * C_LAT
F32 = jnp.float32
BF16 = jnp.bfloat16
VMEM = pl.BlockSpec(memory_space=pltpu.VMEM)
HBM = pl.BlockSpec(memory_space=pltpu.HBM)


def place_code(index):
    return ((index & 127) + 128) << (index >> 7)


def select(picks, values):
    return lax.dot_general(picks, values, (((1,), (1,)), ((), ())), preferred_element_type=F32)


def pack_kernel(devices, rows, half, cells_ref, latents_ref, out_ref):
    count = latents_ref.shape[1]
    tokens = -(-count // 128) * 128
    cells = cells_ref[...].reshape(1, count)
    latents = latents_ref[...]
    if tokens > count:
        cells = jnp.concatenate([cells, jnp.full((1, tokens - count), 1 << 20, jnp.int32)], 1)
        latents = jnp.concatenate(
            [latents, jnp.zeros((latents.shape[0], tokens - count), latents.dtype)], 1
        )
    column = lax.rem(cells, HALF_W)
    token_row = lax.rem(lax.div(cells, HALF_W), HALF_ROWS * HBANDS)
    frame = lax.div(cells, HALF_W * HALF_ROWS * HBANDS)
    block = lax.div(frame, TB)
    band = lax.div(token_row, HALF_ROWS)
    side = lax.rem(token_row, HALF_ROWS)
    local = (lax.rem(frame, TB) * HALF_ROWS + side) * HALF_W + column
    code = place_code((lax.rem(block, 3) * 3 + lax.rem(band, 3)) * TILE_TOKENS + local)
    code = code.astype(F32)

    device = lax.broadcasted_iota(jnp.int32, (devices, tokens), 0)
    tile = lax.rem(device + OFFSET, devices)
    to_band = lax.rem(tile, HBANDS)
    age = lax.div(tile, HBANDS) - block
    near = (
        (band == to_band)
        | ((band == to_band - 1) & (side == HALF_ROWS - 1))
        | ((band == to_band + 1) & (side == 0))
    )
    hits = jnp.where((age >= 0) & (age < 3) & near, 1.0, 0.0)
    before = lax.broadcasted_iota(jnp.int32, (tokens, tokens), 0) < lax.broadcasted_iota(
        jnp.int32, (tokens, tokens), 1
    )
    before = jnp.where(before, 1.0, 0.0).astype(BF16)
    rank = jnp.dot(hits.astype(BF16), before, preferred_element_type=F32)
    rank = jnp.where(hits > 0.5, rank, -1.0)

    slot = lax.broadcasted_iota(jnp.int32, (rows, tokens), 0).astype(F32)
    low_slot = jnp.where(slot < half, slot, -7.0)
    high_slot = jnp.where(slot < half, slot + half, -7.0)
    low = jnp.concatenate(
        [jnp.where(rank[d : d + 1] == low_slot, 1.0, 0.0).astype(BF16) for d in range(devices)], 0
    )
    high = jnp.concatenate(
        [jnp.where(rank[d : d + 1] == high_slot, 1.0, 0.0).astype(BF16) for d in range(devices)], 0
    )
    blank = jnp.zeros_like(latents)
    codes = jnp.broadcast_to(code, (128, tokens)).astype(BF16)
    low_out = select(low, jnp.concatenate([latents, blank, codes], 0))
    high_out = select(high, jnp.concatenate([blank, latents, codes], 0))
    row = lax.broadcasted_iota(jnp.int32, (rows, 128), 0)
    diagonal = row == lax.broadcasted_iota(jnp.int32, (rows, 128), 1)
    for d in range(devices):
        part = slice(d * rows, (d + 1) * rows)
        low_codes = jnp.sum(jnp.where(diagonal, low_out[part, 128:], 0.0), 0, keepdims=True)
        high_codes = jnp.sum(jnp.where(diagonal, high_out[part, 128:], 0.0), 0, keepdims=True)
        body = low_out[part, :128] + high_out[part, :128]
        body = jnp.where(row == rows - 2, low_codes, body)
        body = jnp.where(row == rows - 1, high_codes, body)
        out_ref[part, :] = body.astype(BF16)


def weight_kernel(w_ref, sums_ref):
    first, middle, last = (w_ref[t].astype(F32) * 0.5 for t in range(3))
    outer = first + last
    sums_ref[0] = (outer + middle).astype(BF16)
    sums_ref[1] = (outer - middle).astype(BF16)


def main_kernel(
    devices,
    blocks,
    arrived_ref,
    w_in_ref,
    b_in_ref,
    gain_ref,
    w_mid_hbm,
    w_sum_hbm,
    b_mid_ref,
    out_hbm,
    w_mid_ref,
    edge_ref,
    active_ref,
    mixed_ref,
    hidden_ref,
    sums_ref,
    mix_ref,
    out_ref,
    w_sem,
    out_sem,
):
    copies = [
        pltpu.make_async_copy(source, w_mid_ref.at[k], w_sem.at[k])
        for k, source in (
            (1, w_sum_hbm.at[0]),
            (2, w_sum_hbm.at[1]),
            (0, w_mid_hbm.at[0]),
            (3, w_mid_hbm.at[2]),
        )
    ]
    for copy in copies:
        copy.start()
    total = arrived_ref.shape[0]
    rows = total // devices
    c_mid = gain_ref.shape[0]
    tile = lax.rem(lax.axis_index("sp") + OFFSET, devices)
    band = lax.rem(tile, HBANDS)
    time_block = lax.div(tile, HBANDS)

    arrived = arrived_ref[...]
    low_codes = jnp.concatenate(
        [arrived[(s + 1) * rows - 2 : (s + 1) * rows - 1, :rows] for s in range(devices)], 1
    ).astype(F32)
    high_codes = jnp.concatenate(
        [arrived[(s + 1) * rows - 1 : (s + 1) * rows, :rows] for s in range(devices)], 1
    ).astype(F32)
    k = lax.broadcasted_iota(jnp.int32, (128, 256), 0)
    lane = lax.broadcasted_iota(jnp.int32, (128, 256), 1)
    within = lane & 63
    swap = ((lane >> 6) ^ (lane >> 7)) & 1
    source = swap * (2 * C_LAT) + jnp.where(
        within < C_LAT,
        within + C_LAT,
        jnp.where(within < 3 * C_LAT, within - C_LAT, within - 3 * C_LAT),
    )
    low_spread = jnp.where(k == source, 1.0, 0.0).astype(BF16)
    high_spread = jnp.where(k == source + PATCH, 1.0, 0.0).astype(BF16)
    low_tokens = jnp.dot(arrived, low_spread, preferred_element_type=F32).astype(BF16)
    high_tokens = jnp.dot(arrived, high_spread, preferred_element_type=F32).astype(BF16)

    column = lax.broadcasted_iota(jnp.int32, (HALF_W, 1), 0)
    lanes = lax.broadcasted_iota(jnp.int32, (1, 1, 256), 2) & 63
    from_left, from_right = lanes < C_LAT, lanes >= 3 * C_LAT
    first = lax.broadcasted_iota(jnp.int32, (1, 1, 128), 2) < PATCH
    token_rows = HALF_ROWS + 2
    for f in range(TB * blocks):
        low_pick, high_pick = [], []
        frame = (time_block - (blocks - 1)) * TB + f
        for i in range(token_rows):
            token_row = band * HALF_ROWS - 1 + i
            valid = (frame >= 0) & (token_row >= 0) & (token_row < HALF_ROWS * HBANDS)
            frame_in = lax.max(frame, 0)
            row_in = lax.max(token_row, 0)
            base = (
                lax.rem(lax.div(frame_in, TB), 3) * 3 + lax.rem(lax.div(row_in, HALF_ROWS), 3)
            ) * TILE_TOKENS + (
                lax.rem(frame_in, TB) * HALF_ROWS + lax.rem(row_in, HALF_ROWS)
            ) * HALF_W
            code = jnp.where(valid, place_code(base + column), -1).astype(F32)
            low_pick.append(jnp.where(low_codes == code, 1.0, 0.0).astype(BF16))
            high_pick.append(jnp.where(high_codes == code, 1.0, 0.0).astype(BF16))
        placed = jnp.dot(
            jnp.concatenate(low_pick, 0), low_tokens, preferred_element_type=F32
        ) + jnp.dot(jnp.concatenate(high_pick, 0), high_tokens, preferred_element_type=F32)
        placed = placed.reshape(token_rows, HALF_W, 256)
        gap = jnp.zeros((token_rows, 1, 256), F32)
        left = jnp.concatenate([gap, placed[:, :-1]], 1)
        right = jnp.concatenate([placed[:, 1:], gap], 1)
        placed = jnp.where(from_left, left, jnp.where(from_right, right, placed))
        even_rows, odd_rows = placed[:, :, :128], placed[:, :, 128:]
        below = jnp.concatenate([odd_rows[1:], jnp.zeros((1, HALF_W, 128), F32)], 0)
        odd_rows = jnp.where(first, odd_rows, below)
        for i in range(token_rows):
            start = 2 * i * HALF_W
            edge_ref[f, start : start + HALF_W, :] = even_rows[i].astype(BF16)
            edge_ref[f, start + HALF_W : start + 2 * HALF_W, :] = odd_rows[i].astype(BF16)

    wide = (HB + 2) * HALF_W
    index = lax.broadcasted_iota(jnp.int32, (wide, 1), 0)
    global_row = band * HB - 1 + lax.div(index, HALF_W)
    inside = (global_row >= 0) & (global_row < HB * HBANDS)
    bias = b_in_ref[...].reshape(1, c_mid)
    gain = gain_ref[...].reshape(1, c_mid)
    bias_mid = b_mid_ref[...].reshape(1, c_mid)

    def activate(a):
        windows, kernels = [], []
        for tap in range(3):
            f = TB * (blocks - 1) - 4 + a + tap
            if f < 0:
                continue
            windows += [
                edge_ref[f, 0:wide, :],
                edge_ref[f, 2 * HALF_W : 2 * HALF_W + wide, :],
            ]
            kernels.append(w_in_ref[tap])
        sums = jnp.dot(
            jnp.concatenate(windows, 1), jnp.concatenate(kernels, 0), preferred_element_type=F32
        )
        keep = inside & (time_block * TB - 2 + a >= 0)
        for p in range(2):
            part = slice(p * c_mid, (p + 1) * c_mid)
            hidden = (sums[:, part] + bias).astype(BF16)
            if a >= 2:
                hidden_ref[a - 2, :, part] = hidden[HALF_W : HALF_W + HB * HALF_W]
            values = hidden.astype(F32)
            mean = jnp.sum(values * values, 1, keepdims=True) * (1.0 / c_mid)
            inverse = jnp.where(keep, lax.rsqrt(mean + 1e-06) * 0.5, 0.0)
            halved = values * inverse * gain
            active_ref[a, :, part] = (halved + halved * jnp.tanh(halved)).astype(BF16)

    tall = HB * HALF_W

    def product(k):
        if k == 0:
            mixed_ref[k] = active_ref[0] - active_ref[2]
        elif k == 1:
            mixed_ref[k] = active_ref[1] + active_ref[2]
        elif k == 2:
            mixed_ref[k] = active_ref[2] - active_ref[1]
        else:
            mixed_ref[k] = active_ref[1] - active_ref[3]
        windows, kernels = [], []
        evens, odds, rights, lefts = [], [], [], []
        for tap_row in range(3):
            rows_in = slice(tap_row * HALF_W, tap_row * HALF_W + tall)
            windows.append(mixed_ref[k, rows_in, :])
            w0, w1, w2 = (w_mid_ref[k, tap_row, t] for t in range(3))
            kernels.append(jnp.concatenate([w1, w0], 1))
            kernels.append(jnp.concatenate([w2, w1], 1))
            evens.append(mixed_ref[k, rows_in, :c_mid])
            odds.append(mixed_ref[k, rows_in, c_mid:])
            rights.append(w2)
            lefts.append(w0)
        return (
            jnp.dot(
                jnp.concatenate(windows, 1),
                jnp.concatenate(kernels, 0),
                preferred_element_type=F32,
            ),
            jnp.dot(
                jnp.concatenate(evens, 1), jnp.concatenate(rights, 0), preferred_element_type=F32
            ),
            jnp.dot(
                jnp.concatenate(odds, 1), jnp.concatenate(lefts, 0), preferred_element_type=F32
            ),
        )

    def finish(o, sums, from_even, from_odd):
        gap = jnp.zeros((HB, 1, c_mid), F32)
        from_even = from_even.reshape(HB, HALF_W, c_mid)
        from_odd = from_odd.reshape(HB, HALF_W, c_mid)
        to_odd = jnp.concatenate([from_even[:, 1:], gap], 1).reshape(tall, c_mid)
        to_even = jnp.concatenate([gap, from_odd[:, :-1]], 1).reshape(tall, c_mid)
        hidden = hidden_ref[o].astype(F32)
        even_out = sums[:, :c_mid] + to_even + bias_mid + hidden[:, :c_mid]
        odd_out = sums[:, c_mid:] + to_odd + bias_mid + hidden[:, c_mid:]
        for g in range(c_mid // 128):
            part = slice(g * 128, (g + 1) * 128)
            mix_ref[g, pl.ds(0, tall, stride=2), :] = even_out[:, part]
            mix_ref[g, pl.ds(1, tall, stride=2), :] = odd_out[:, part]
            out_ref[o, :, part] = mix_ref[g].astype(BF16)
        copy = pltpu.make_async_copy(
            out_ref.at[o], out_hbm.at[pl.ds(o * 2 * tall, 2 * tall), :], out_sem.at[o]
        )
        copy.start()
        return copy

    pieces = (slice(0, 2 * c_mid), slice(2 * c_mid, 3 * c_mid), slice(3 * c_mid, 4 * c_mid))
    activate(1)
    activate(2)
    copies[0].wait()
    for piece, value in zip(pieces, product(1)):
        sums_ref[0, :, piece] = value
    activate(0)
    copies[1].wait()
    for piece, value in zip(pieces, product(2)):
        earlier = sums_ref[0, :, piece]
        sums_ref[0, :, piece] = earlier + value
        sums_ref[1, :, piece] = earlier - value
    activate(3)
    copies[2].wait()
    first = finish(0, *(sums_ref[0, :, p] + v for p, v in zip(pieces, product(0))))
    copies[3].wait()
    last = finish(1, *(sums_ref[1, :, p] - v for p, v in zip(pieces, product(3))))
    first.wait()
    last.wait()


def input_kernel(w_in):
    c_mid = w_in.shape[-1]
    gap = jnp.zeros((3, 3, 1) + w_in.shape[3:], w_in.dtype)
    even = jnp.concatenate([w_in, gap], 2)
    odd = jnp.concatenate([gap, w_in], 2)
    both = jnp.concatenate([even, odd], -1).reshape(3, 3 * PATCH, 2 * c_mid)
    return jnp.pad(both, ((0, 0), (0, PATCH), (0, 0)))


def shards(latents, row_cell, w_in, b_in, gain, w_mid, b_mid):
    devices = lax.axis_size("sp")
    tokens = latents.shape[0]
    c_mid = gain.shape[0]
    blocks = min(3, devices // HBANDS)
    pair = tokens // devices
    slots = pair * 3 * blocks + pair
    half = -(-slots // 2)
    rows = -(-(half + 2) // 8) * 8
    outgoing = pl.pallas_call(
        functools.partial(pack_kernel, devices, rows, half),
        out_shape=jax.ShapeDtypeStruct((devices * rows, 128), BF16),
        in_specs=[VMEM, VMEM],
        out_specs=VMEM,
        name="pack",
    )(row_cell, latents.T)
    arrived = lax.all_to_all(
        outgoing.reshape(devices, rows, 128), "sp", split_axis=0, concat_axis=0, tiled=True
    )
    taps = pl.BlockSpec((3, 1, 1, c_mid, c_mid), lambda i, j: (0, i, j, 0, 0))
    w_sum = pl.pallas_call(
        weight_kernel,
        grid=(3, 3),
        out_shape=jax.ShapeDtypeStruct((2, 3, 3, c_mid, c_mid), BF16),
        in_specs=[taps],
        out_specs=pl.BlockSpec((2, 1, 1, c_mid, c_mid), lambda i, j: (0, i, j, 0, 0)),
        name="weights",
    )(w_mid)
    wide = (HB + 2) * HALF_W
    decoded = pl.pallas_call(
        functools.partial(main_kernel, devices, blocks),
        out_shape=jax.ShapeDtypeStruct((TB * HB * W, c_mid), BF16),
        in_specs=[VMEM, VMEM, VMEM, VMEM, HBM, HBM, VMEM],
        out_specs=HBM,
        scratch_shapes=[
            pltpu.VMEM((4, 3, 3, c_mid, c_mid), BF16),
            pltpu.VMEM((TB * blocks, 2 * (HALF_ROWS + 2) * HALF_W, 128), BF16),
            pltpu.VMEM((TB + 2, wide, 2 * c_mid), BF16),
            pltpu.VMEM((4, wide, 2 * c_mid), BF16),
            pltpu.VMEM((TB, HB * HALF_W, 2 * c_mid), BF16),
            pltpu.VMEM((2, HB * HALF_W, 4 * c_mid), F32),
            pltpu.VMEM((c_mid // 128, HB * W, 128), F32),
            pltpu.VMEM((TB, HB * W, c_mid), BF16),
            pltpu.SemaphoreType.DMA((4,)),
            pltpu.SemaphoreType.DMA((TB,)),
        ],
        compiler_params=pltpu.CompilerParams(vmem_limit_bytes=48 * 1024 * 1024),
        name="block",
    )(
        arrived.reshape(devices * rows, 128),
        input_kernel(w_in),
        b_in,
        gain,
        w_mid,
        w_sum,
        b_mid,
    )
    return decoded.reshape(1, TB, HB, W, c_mid)


def solution(mesh):
    return jax.shard_map(
        shards,
        mesh=mesh,
        in_specs=(P(("grp", "sp"), None), P(("grp", "sp")), P(), P(), P(), P(), P()),
        out_specs=P(("grp", "sp"), None, None, None, None),
        check_vma=False,
    )
```

```python
import functools

import jax
import jax.numpy as jnp
from jax import lax
from jax.experimental import pallas as pl
from jax.experimental.pallas import tpu as pltpu
from jax.sharding import PartitionSpec as P

C_LAT = 16
W = 160
TB = 2
HBANDS = 8
HB = 4
OFFSET = 2 * HBANDS + HBANDS // 2
HALF_ROWS = HB // 2
HALF_W = W // 2
TILE_TOKENS = TB * HALF_ROWS * HALF_W
PATCH = 4 * C_LAT
GROUP = 1
F32 = jnp.float32
BF16 = jnp.bfloat16
VMEM = pl.BlockSpec(memory_space=pltpu.VMEM)
HBM = pl.BlockSpec(memory_space=pltpu.HBM)


def place_code(index):
    return ((index & 127) + 128) << (index >> 7)


def select(picks, values):
    return lax.dot_general(picks, values, (((1,), (1,)), ((), ())), preferred_element_type=F32)


def pack_kernel(devices, rows, half, slots, cells_ref, latents_ref, out_ref):
    chips = devices // GROUP
    count = latents_ref.shape[1]
    tokens = -(-count // 128) * 128
    cells = cells_ref[...].reshape(1, count)
    latents = latents_ref[...]
    if tokens > count:
        cells = jnp.concatenate([cells, jnp.full((1, tokens - count), 1 << 20, jnp.int32)], 1)
        latents = jnp.concatenate(
            [latents, jnp.zeros((latents.shape[0], tokens - count), latents.dtype)], 1
        )
    column = lax.rem(cells, HALF_W)
    token_row = lax.rem(lax.div(cells, HALF_W), HALF_ROWS * HBANDS)
    frame = lax.div(cells, HALF_W * HALF_ROWS * HBANDS)
    block = lax.div(frame, TB)
    band = lax.div(token_row, HALF_ROWS)
    side = lax.rem(token_row, HALF_ROWS)
    local = (lax.rem(frame, TB) * HALF_ROWS + side) * HALF_W + column
    code = place_code((lax.rem(block, 3) * 3 + lax.rem(band, 3)) * TILE_TOKENS + local)
    code = code.astype(F32)

    chip = lax.broadcasted_iota(jnp.int32, (chips, tokens), 0)
    tile = lax.rem(chip * GROUP + OFFSET, devices)
    top = lax.rem(tile, HBANDS)
    bottom = top + GROUP - 1
    age = lax.div(tile, HBANDS) - block
    near = (
        ((band >= top) & (band <= bottom))
        | ((band == top - 1) & (side == HALF_ROWS - 1))
        | ((band == bottom + 1) & (side == 0))
    )
    own = jnp.where(near & (age == 0), 1.0, 0.0)
    old = jnp.where(near & (age > 0) & (age < 3), 1.0, 0.0)
    before = lax.broadcasted_iota(jnp.int32, (tokens, tokens), 0) < lax.broadcasted_iota(
        jnp.int32, (tokens, tokens), 1
    )
    before = jnp.where(before, 1.0, 0.0).astype(BF16)
    ranks = jnp.dot(
        jnp.concatenate([own, old], 0).astype(BF16), before, preferred_element_type=F32
    )
    rank = jnp.where(
        own > 0.5, ranks[:chips], jnp.where(old > 0.5, slots - 1 - ranks[chips:], -1.0)
    )

    slot = lax.broadcasted_iota(jnp.int32, (rows, tokens), 0).astype(F32)
    low_slot = jnp.where(slot < half, slot, -7.0)
    high_slot = jnp.where(slot < half, slot + half, -7.0)
    blank = jnp.zeros_like(latents)
    codes = jnp.broadcast_to(code, (128, tokens)).astype(BF16)
    low_values = jnp.concatenate([latents, blank, codes], 0)
    high_values = jnp.concatenate([blank, latents, codes], 0)
    low_out = select(
        jnp.concatenate(
            [jnp.where(rank[d : d + 1] == low_slot, 1.0, 0.0).astype(BF16) for d in range(chips)], 0
        ),
        low_values,
    )
    high_out = select(
        jnp.concatenate(
            [jnp.where(rank[d : d + 1] == high_slot, 1.0, 0.0).astype(BF16) for d in range(chips)],
            0,
        ),
        high_values,
    )
    row = lax.broadcasted_iota(jnp.int32, (rows, 128), 0)
    diagonal = row == lax.broadcasted_iota(jnp.int32, (rows, 128), 1)
    for d in range(chips):
        part = slice(d * rows, (d + 1) * rows)
        low_codes = jnp.sum(jnp.where(diagonal, low_out[part, 128:], 0.0), 0, keepdims=True)
        high_codes = jnp.sum(jnp.where(diagonal, high_out[part, 128:], 0.0), 0, keepdims=True)
        body = low_out[part, :128] + high_out[part, :128]
        body = jnp.where(row == rows - 2, low_codes, body)
        body = jnp.where(row == rows - 1, high_codes, body)
        out_ref[part, :] = body.astype(BF16)


def weight_kernel(w_ref, sums_ref):
    first, middle, last = (w_ref[t].astype(F32) * 0.5 for t in range(3))
    outer = first + last
    sums_ref[0] = (outer + middle).astype(BF16)
    sums_ref[1] = (outer - middle).astype(BF16)


def slot_pieces(first, last, half, rows):
    pieces = []
    for high, start, stop in (
        (0, first, min(last, half)),
        (1, max(first, half) - half, last - half),
    ):
        if start < stop:
            pieces.append((high, start // 8 * 8, min(rows, -(-stop // 8) * 8)))
    return pieces


def run(*lists):
    steps = []
    for which, steps_of in enumerate(lists):
        for i, step in enumerate(steps_of):
            steps.append(((i + 0.5) / len(steps_of), which, i, step))
    for step in sorted(steps, key=lambda entry: entry[:3]):
        step[3]()


def main_kernel(
    devices,
    blocks,
    rows,
    half,
    own_slots,
    old_slots,
    slots,
    arrived_ref,
    w_in_ref,
    b_in_ref,
    gain_ref,
    w_mid_hbm,
    w_sum_hbm,
    b_mid_ref,
    out_hbm,
    w_mid_ref,
    spread_ref,
    picked_ref,
    placed_ref,
    edge_ref,
    input_ref,
    active_ref,
    mixed_ref,
    hidden_ref,
    sums_ref,
    mix_ref,
    out_ref,
    w_sem,
    out_sem,
):
    def fetch(k, r):
        source, t = ((w_mid_hbm, 0), (w_sum_hbm, 0), (w_sum_hbm, 1), (w_mid_hbm, 2))[k]
        return pltpu.make_async_copy(source.at[t, r], w_mid_ref.at[k, r], w_sem.at[k, r])

    def start_rows(k):
        def body(r, carry):
            fetch(k, r).start()
            return carry

        lax.fori_loop(0, 3, body, 0)

    def wait_rows(k):
        for r in range(3):
            fetch(k, r).wait()

    for k in (1, 0, 2, 3):
        start_rows(k)
    chips = devices // GROUP
    c_mid = gain_ref.shape[0]
    tile = lax.rem(lax.axis_index("sp") + OFFSET, devices)
    band = lax.rem(tile, HBANDS)
    time_block = lax.div(tile, HBANDS)
    token_rows = HALF_ROWS + 2
    wide = (HB + 2) * HALF_W
    tall = HB * HALF_W

    blank = jnp.zeros((C_LAT, c_mid), BF16)
    for tap in range(3):
        for tap_row in range(4):
            for spot in range(4):
                at = slice(tap_row * PATCH + spot * C_LAT, tap_row * PATCH + (spot + 1) * C_LAT)
                even = w_in_ref[tap, tap_row, spot] if tap_row < 3 and spot < 3 else blank
                odd = w_in_ref[tap, tap_row, spot - 1] if tap_row < 3 and spot > 0 else blank
                spread_ref[tap, at, :c_mid] = even
                spread_ref[tap, at, c_mid:] = odd

    k = lax.broadcasted_iota(jnp.int32, (256, 256), 0)
    lane = lax.broadcasted_iota(jnp.int32, (256, 256), 1)
    within = lane & 63
    swap = ((lane >> 6) ^ (lane >> 7)) & 1
    source = swap * (2 * C_LAT) + jnp.where(
        within < C_LAT,
        within + C_LAT,
        jnp.where(within < 3 * C_LAT, within - C_LAT, within - 3 * C_LAT),
    )
    layout = jnp.where((k == source) | (k == source + 128 + PATCH), 1.0, 0.0).astype(BF16)

    def arrivals(pieces):
        codes, tokens = {}, {}
        for high, start, stop in pieces:
            code_row = rows - 2 + high
            codes[high] = jnp.concatenate(
                [
                    arrived_ref[s * rows + code_row : s * rows + code_row + 1, start:stop]
                    for s in range(chips)
                ],
                1,
            ).astype(F32)
            if stop - start == rows:
                parts = [arrived_ref[...]]
            else:
                parts = [
                    arrived_ref[s * rows + start : s * rows + stop, :]
                    for s in range(chips)
                ]
            tokens[high] = jnp.concatenate(parts, 0)
        return codes, tokens

    by_age = [arrivals(slot_pieces(0, own_slots, half, rows))]
    if blocks > 1:
        by_age.append(arrivals(slot_pieces(slots - old_slots, slots, half, rows)))

    column = lax.broadcasted_iota(jnp.int32, (HALF_W, 1), 0)
    lanes = lax.broadcasted_iota(jnp.int32, (1, 1, 256), 2) & 63
    from_left, from_right = lanes < C_LAT, lanes >= 3 * C_LAT
    upper = lax.broadcasted_iota(jnp.int32, (1, 1, 128), 2) < PATCH

    def picks(f):
        if f < 0:
            return []
        frame = (time_block - (blocks - 1)) * TB + f
        codes, tokens = by_age[0 if f >= TB * (blocks - 1) else 1]

        def pick(start, stop):
            def step():
                picked = {}
                for high in codes:
                    picks = []
                    for i in range(start, stop):
                        token_row = band * HALF_ROWS - 1 + i
                        valid = (
                            (frame >= 0) & (token_row >= 0) & (token_row < HALF_ROWS * HBANDS)
                        )
                        frame_in = lax.max(frame, 0)
                        row_in = lax.max(token_row, 0)
                        base = (
                            lax.rem(lax.div(frame_in, TB), 3) * 3
                            + lax.rem(lax.div(row_in, HALF_ROWS), 3)
                        ) * TILE_TOKENS + (
                            lax.rem(frame_in, TB) * HALF_ROWS + lax.rem(row_in, HALF_ROWS)
                        ) * HALF_W
                        code = jnp.where(valid, place_code(base + column), -1).astype(F32)
                        picks.append(jnp.where(codes[high] == code, 1.0, 0.0).astype(BF16))
                    picked[high] = jnp.dot(
                        jnp.concatenate(picks, 0), tokens[high], preferred_element_type=F32
                    ).astype(BF16)
                    picked_ref[f, start * HALF_W : stop * HALF_W, high * 128 : high * 128 + 128] = (
                        picked[high]
                    )
                for high in range(2):
                    if high not in codes:
                        picked_ref[
                            f, start * HALF_W : stop * HALF_W, high * 128 : high * 128 + 128
                        ] = jnp.zeros(((stop - start) * HALF_W, 128), BF16)

            return step

        return [pick(0, token_rows // 2), pick(token_rows // 2, token_rows)]

    def edges(f):
        if f < 0:
            return []

        def spread():
            placed_ref[f] = jnp.dot(picked_ref[f], layout, preferred_element_type=F32)

        def shift():
            placed = placed_ref[f].reshape(token_rows, HALF_W, 256)
            gap = jnp.zeros((token_rows, 1, 256), F32)
            left = jnp.concatenate([gap, placed[:, :-1]], 1)
            right = jnp.concatenate([placed[:, 1:], gap], 1)
            placed = jnp.where(from_left, left, jnp.where(from_right, right, placed))
            even_rows, odd_rows = placed[:, :, :128], placed[:, :, 128:]
            below = jnp.concatenate([odd_rows[1:], jnp.zeros((1, HALF_W, 128), F32)], 0)
            odd_rows = jnp.where(upper, odd_rows, below)
            for i in range(token_rows):
                start = 2 * i * HALF_W
                edge_ref[f, start : start + HALF_W, :] = even_rows[i].astype(BF16)
                edge_ref[f, start + HALF_W : start + 2 * HALF_W, :] = odd_rows[i].astype(BF16)

        return [spread, shift]

    index = lax.broadcasted_iota(jnp.int32, (HALF_W, 1), 0)
    bias = b_in_ref[...].reshape(1, c_mid)
    gain = gain_ref[...].reshape(1, c_mid)
    bias_mid = b_mid_ref[...].reshape(1, c_mid)

    def convolved(a):
        def convolve(part):
            def step():
                windows, kernels = [], []
                for tap in range(3):
                    f = TB * (blocks - 1) - 4 + a + tap
                    if f < 0:
                        continue
                    windows += [
                        edge_ref[f, 0:wide, :],
                        edge_ref[f, 2 * HALF_W : 2 * HALF_W + wide, :],
                    ]
                    kernels.append(spread_ref[tap, :, part])
                input_ref[a, :, part] = jnp.dot(
                    jnp.concatenate(windows, 1),
                    jnp.concatenate(kernels, 0),
                    preferred_element_type=F32,
                )

            return step

        return [convolve(slice(n, n + 256)) for n in range(0, 2 * c_mid, 256)]

    def activated(a):
        def normalise(r, p):
            def step():
                part = slice(p * c_mid, (p + 1) * c_mid)
                at = slice(r * HALF_W, (r + 1) * HALF_W)
                hidden = (input_ref[a, at, part] + bias).astype(BF16)
                if a >= 2 and 1 <= r <= HB:
                    hidden_ref[a - 2, (r - 1) * HALF_W : r * HALF_W, part] = hidden
                values = hidden.astype(F32)
                mean = jnp.sum(values * values, 1, keepdims=True) * (1.0 / c_mid)
                inverse = lax.rsqrt(mean + 1e-06) * 0.5
                keep = time_block * TB - 2 + a >= 0
                if r in (0, HB + 1):
                    row = band * HB - 1 + r
                    keep = keep & (row >= 0) & (row < HB * HBANDS)
                halved = values * jnp.where(keep, inverse, 0.0) * gain
                active_ref[a, at, part] = (halved + halved * jnp.tanh(halved)).astype(BF16)

            return step

        return [normalise(r, p) for r in range(HB + 2) for p in range(2)]

    halves = 2
    part_rows = tall // halves

    def mix(k):
        def rows_of(start):
            def step():
                at = slice(start, start + 2 * HALF_W)
                one, two, sign = ((0, 2, -1), (1, 2, 1), (2, 1, -1), (1, 3, -1))[k]
                first, second = active_ref[one, at, :], active_ref[two, at, :]
                mixed_ref[k, at, :] = first + second if sign > 0 else first - second

            return step

        return [rows_of(start) for start in range(0, wide, 2 * HALF_W)]

    def product(k, h):
        def piece(source, part, kernel):
            def step():
                windows = [
                    mixed_ref[k, r * HALF_W + h * part_rows : r * HALF_W + (h + 1) * part_rows, source]
                    for r in range(3)
                ]
                value = jnp.dot(
                    jnp.concatenate(windows, 1), kernel(), preferred_element_type=F32
                )
                at = slice(h * part_rows, (h + 1) * part_rows)
                if k == 1:
                    sums_ref[1, at, part] = value
                elif k == 0:
                    sums_ref[0, at, part] = sums_ref[1, at, part] + value
                elif k == 2:
                    sums_ref[0, at, part] = sums_ref[0, at, part] + value
                    sums_ref[1, at, part] = sums_ref[1, at, part] - value
                else:
                    sums_ref[1, at, part] = sums_ref[1, at, part] - value

            return step

        def taps(column_tap, start, stop):
            return [w_mid_ref[k, r, column_tap, :, start:stop] for r in range(3)]

        def straight(start, stop):
            def kernel():
                blocks_of = []
                for r in range(3):
                    for even_tap, odd_tap in ((1, 0), (2, 1)):
                        columns = []
                        if start < c_mid:
                            columns.append(
                                w_mid_ref[k, r, even_tap, :, start : min(stop, c_mid)]
                            )
                        if stop > c_mid:
                            columns.append(
                                w_mid_ref[k, r, odd_tap, :, max(start, c_mid) - c_mid : stop - c_mid]
                            )
                        blocks_of.append(
                            columns[0] if len(columns) == 1 else jnp.concatenate(columns, 1)
                        )
                return jnp.concatenate(blocks_of, 0)

            return kernel

        def side(column_tap, start, stop):
            return lambda: jnp.concatenate(taps(column_tap, start, stop), 0)

        steps = [
            piece(slice(0, 2 * c_mid), slice(n, n + 256), straight(n, n + 256))
            for n in range(0, 2 * c_mid, 256)
        ]
        for p, column_tap in ((0, 2), (1, 0)):
            for start in range(0, c_mid, 256):
                stop = min(start + 256, c_mid)
                at = (2 + p) * c_mid
                steps.append(
                    piece(
                        slice(p * c_mid, (p + 1) * c_mid),
                        slice(at + start, at + stop),
                        side(column_tap, start, stop),
                    )
                )
        return steps

    def finish(o, h):
        out_rows = 2 * part_rows

        def lane_group(g):
            def step():
                at = slice(h * part_rows, (h + 1) * part_rows)

                def piece(which):
                    start = which * c_mid + g * 128
                    return sums_ref[o, at, start : start + 128]

                gap = jnp.zeros((HB // halves, 1, 128), F32)
                shape = (HB // halves, HALF_W, 128)
                to_odd = jnp.concatenate([piece(2).reshape(shape)[:, 1:], gap], 1)
                to_even = jnp.concatenate([gap, piece(3).reshape(shape)[:, :-1]], 1)
                lanes_of = slice(g * 128, (g + 1) * 128)
                for p, moved in ((0, to_even), (1, to_odd)):
                    start = p * c_mid + g * 128
                    hidden = hidden_ref[o, at, start : start + 128].astype(F32)
                    mix_ref[o, h, g, pl.ds(p, part_rows, stride=2), :] = (
                        piece(p) + moved.reshape(part_rows, 128) + bias_mid[:, lanes_of] + hidden
                    )
                out_ref[o, h * out_rows : (h + 1) * out_rows, lanes_of] = mix_ref[o, h, g].astype(
                    BF16
                )

            return step

        def send():
            leave(o, h).start()

        return [lane_group(g) for g in range(c_mid // 128)] + [send]

    def leave(o, h):
        out_rows = 2 * part_rows
        return pltpu.make_async_copy(
            out_ref.at[o, pl.ds(h * out_rows, out_rows), :],
            out_hbm.at[pl.ds(o * 2 * tall + h * out_rows, out_rows), :],
            out_sem.at[o, h],
        )

    newest = TB * (blocks - 1) - 2
    for f in range(newest):
        run(picks(f) + edges(f))
    run(picks(newest) + picks(newest + 1))
    run(edges(newest), picks(newest + 2))
    run(edges(newest + 1) + convolved(1), picks(newest + 3))
    run(edges(newest + 2) + convolved(2), activated(1))
    run(edges(newest + 3) + convolved(0) + convolved(3), activated(2))
    wait_rows(1)
    wait_rows(0)
    run(mix(1))
    run(product(1, 0) + product(1, 1), activated(0) + mix(0))
    run(product(0, 0) + product(0, 1), mix(2))
    wait_rows(2)
    wait_rows(3)
    run(product(2, 0) + product(2, 1), activated(3) + mix(3))
    run(product(3, 0), finish(0, 0) + finish(0, 1))
    run(product(3, 1), finish(1, 0))
    run(finish(1, 1))
    for o in range(TB):
        for h in range(halves):
            leave(o, h).wait()


def shards(latents, row_cell, w_in, b_in, gain, w_mid, b_mid):
    devices = lax.axis_size("sp")
    tokens = latents.shape[0]
    c_mid = gain.shape[0]
    blocks = min(3, devices // HBANDS)
    chips = devices // GROUP
    pair = tokens // devices
    bands = GROUP + 2
    own_slots = pair * bands + pair
    old_slots = pair * bands * (blocks - 1) + pair
    slots = pair * bands * blocks + pair
    half = -(-slots // 2)
    rows = -(-(half + 2) // 8) * 8
    outgoing = pl.pallas_call(
        functools.partial(pack_kernel, devices, rows, half, slots),
        out_shape=jax.ShapeDtypeStruct((chips * rows, 128), BF16),
        in_specs=[VMEM, VMEM],
        out_specs=VMEM,
        name="pack",
    )(row_cell, latents.T)
    arrived = lax.all_to_all(
        outgoing.reshape(chips, rows, 128), "sp", split_axis=0, concat_axis=0, tiled=True
    )
    w_sum = pl.pallas_call(
        weight_kernel,
        grid=(3, 3),
        out_shape=jax.ShapeDtypeStruct((2, 3, 3, c_mid, c_mid), BF16),
        in_specs=[pl.BlockSpec((3, 1, 1, c_mid, c_mid), lambda i, j: (0, i, j, 0, 0))],
        out_specs=pl.BlockSpec((2, 1, 1, c_mid, c_mid), lambda i, j: (0, i, j, 0, 0)),
        name="weights",
    )(w_mid)
    wide = (HB + 2) * HALF_W
    tall = HB * HALF_W
    frames = TB * blocks
    decoded = pl.pallas_call(
        functools.partial(
            main_kernel, devices, blocks, rows, half, own_slots, old_slots, slots
        ),
        out_shape=jax.ShapeDtypeStruct((TB * HB * W, c_mid), BF16),
        in_specs=[VMEM, VMEM, VMEM, VMEM, HBM, HBM, VMEM],
        out_specs=HBM,
        scratch_shapes=[
            pltpu.VMEM((4, 3, 3, c_mid, c_mid), BF16),
            pltpu.VMEM((3, 4 * PATCH, 2 * c_mid), BF16),
            pltpu.VMEM((frames, (HALF_ROWS + 2) * HALF_W, 256), BF16),
            pltpu.VMEM((frames, (HALF_ROWS + 2) * HALF_W, 256), F32),
            pltpu.VMEM((frames, 2 * (HALF_ROWS + 2) * HALF_W, 128), BF16),
            pltpu.VMEM((TB + 2, wide, 2 * c_mid), F32),
            pltpu.VMEM((TB + 2, wide, 2 * c_mid), BF16),
            pltpu.VMEM((4, wide, 2 * c_mid), BF16),
            pltpu.VMEM((TB, tall, 2 * c_mid), BF16),
            pltpu.VMEM((2, tall, 4 * c_mid), F32),
            pltpu.VMEM((TB, 2, c_mid // 128, tall, 128), F32),
            pltpu.VMEM((TB, 2 * tall, c_mid), BF16),
            pltpu.SemaphoreType.DMA((4, 3)),
            pltpu.SemaphoreType.DMA((TB, 2)),
        ],
        compiler_params=pltpu.CompilerParams(vmem_limit_bytes=48 * 1024 * 1024),
        name="block",
    )(
        arrived.reshape(chips * rows, 128),
        w_in,
        b_in,
        gain,
        w_mid,
        pltpu.with_memory_space_constraint(w_sum, pltpu.HBM),
        b_mid,
    )
    return decoded.reshape(1, TB, HB, W, c_mid)


def solution(mesh):
    return jax.shard_map(
        shards,
        mesh=mesh,
        in_specs=(P(("grp", "sp"), None), P(("grp", "sp")), P(), P(), P(), P(), P()),
        out_specs=P(("grp", "sp"), None, None, None, None),
        check_vma=False,
    )
```

```python
import functools

import jax
import jax.numpy as jnp
from jax import lax
from jax.experimental import pallas as pl
from jax.experimental.pallas import tpu as pltpu
from jax.sharding import PartitionSpec as P

C_LAT = 16
W = 160
TB = 2
HBANDS = 8
HB = 4
OFFSET = 2 * HBANDS + HBANDS // 2
HALF_ROWS = HB // 2
HALF_W = W // 2
TILE_TOKENS = TB * HALF_ROWS * HALF_W
PATCH = 4 * C_LAT
GROUP = 1
F32 = jnp.float32
BF16 = jnp.bfloat16
VMEM = pl.BlockSpec(memory_space=pltpu.VMEM)
HBM = pl.BlockSpec(memory_space=pltpu.HBM)


def place_code(index):
    return ((index & 127) + 128) << (index >> 7)


def select(picks, values):
    return lax.dot_general(picks, values, (((1,), (1,)), ((), ())), preferred_element_type=F32)


def pack_kernel(devices, rows, half, slots, cells_ref, latents_ref, out_ref):
    chips = devices // GROUP
    count = latents_ref.shape[1]
    tokens = -(-count // 128) * 128
    cells = cells_ref[...].reshape(1, count)
    latents = latents_ref[...]
    if tokens > count:
        cells = jnp.concatenate([cells, jnp.full((1, tokens - count), 1 << 20, jnp.int32)], 1)
        latents = jnp.concatenate(
            [latents, jnp.zeros((latents.shape[0], tokens - count), latents.dtype)], 1
        )
    column = lax.rem(cells, HALF_W)
    token_row = lax.rem(lax.div(cells, HALF_W), HALF_ROWS * HBANDS)
    frame = lax.div(cells, HALF_W * HALF_ROWS * HBANDS)
    block = lax.div(frame, TB)
    band = lax.div(token_row, HALF_ROWS)
    side = lax.rem(token_row, HALF_ROWS)
    local = (lax.rem(frame, TB) * HALF_ROWS + side) * HALF_W + column
    code = place_code((lax.rem(block, 3) * 3 + lax.rem(band, 3)) * TILE_TOKENS + local)
    code = code.astype(F32)

    chip = lax.broadcasted_iota(jnp.int32, (chips, tokens), 0)
    tile = lax.rem(chip * GROUP + OFFSET, devices)
    top = lax.rem(tile, HBANDS)
    bottom = top + GROUP - 1
    age = lax.div(tile, HBANDS) - block
    near = (
        ((band >= top) & (band <= bottom))
        | ((band == top - 1) & (side == HALF_ROWS - 1))
        | ((band == bottom + 1) & (side == 0))
    )
    own = jnp.where(near & (age == 0), 1.0, 0.0)
    old = jnp.where(near & (age > 0) & (age < 3), 1.0, 0.0)
    before = lax.broadcasted_iota(jnp.int32, (tokens, tokens), 0) < lax.broadcasted_iota(
        jnp.int32, (tokens, tokens), 1
    )
    before = jnp.where(before, 1.0, 0.0).astype(BF16)
    ranks = jnp.dot(
        jnp.concatenate([own, old], 0).astype(BF16), before, preferred_element_type=F32
    )
    rank = jnp.where(
        own > 0.5, ranks[:chips], jnp.where(old > 0.5, slots - 1 - ranks[chips:], -1.0)
    )

    slot = lax.broadcasted_iota(jnp.int32, (rows, tokens), 0).astype(F32)
    low_slot = jnp.where(slot < half, slot, -7.0)
    high_slot = jnp.where(slot < half, slot + half, -7.0)
    blank = jnp.zeros_like(latents)
    codes = jnp.broadcast_to(code, (128, tokens)).astype(BF16)
    low_values = jnp.concatenate([latents, blank, codes], 0)
    high_values = jnp.concatenate([blank, latents, codes], 0)
    low_out = select(
        jnp.concatenate(
            [jnp.where(rank[d : d + 1] == low_slot, 1.0, 0.0).astype(BF16) for d in range(chips)], 0
        ),
        low_values,
    )
    high_out = select(
        jnp.concatenate(
            [jnp.where(rank[d : d + 1] == high_slot, 1.0, 0.0).astype(BF16) for d in range(chips)],
            0,
        ),
        high_values,
    )
    row = lax.broadcasted_iota(jnp.int32, (rows, 128), 0)
    diagonal = row == lax.broadcasted_iota(jnp.int32, (rows, 128), 1)
    for d in range(chips):
        part = slice(d * rows, (d + 1) * rows)
        low_codes = jnp.sum(jnp.where(diagonal, low_out[part, 128:], 0.0), 0, keepdims=True)
        high_codes = jnp.sum(jnp.where(diagonal, high_out[part, 128:], 0.0), 0, keepdims=True)
        body = low_out[part, :128] + high_out[part, :128]
        body = jnp.where(row == rows - 2, low_codes, body)
        body = jnp.where(row == rows - 1, high_codes, body)
        out_ref[part, :] = body.astype(BF16)


def weight_kernel(w_ref, sums_ref):
    first, middle, last = (w_ref[t].astype(F32) * 0.5 for t in range(3))
    outer = first + last
    sums_ref[0] = (outer + middle).astype(BF16)
    sums_ref[1] = (outer - middle).astype(BF16)


def slot_pieces(first, last, half, rows):
    pieces = []
    for high, start, stop in (
        (0, first, min(last, half)),
        (1, max(first, half) - half, last - half),
    ):
        if start < stop:
            pieces.append((high, start // 8 * 8, min(rows, -(-stop // 8) * 8)))
    return pieces


def run(*lists):
    steps = []
    for which, steps_of in enumerate(lists):
        for i, step in enumerate(steps_of):
            steps.append(((i + 0.5) / len(steps_of), which, i, step))
    for step in sorted(steps, key=lambda entry: entry[:3]):
        step[3]()


def main_kernel(
    devices,
    blocks,
    rows,
    half,
    own_slots,
    old_slots,
    slots,
    arrived_ref,
    w_in_ref,
    b_in_ref,
    gain_ref,
    w_mid_hbm,
    w_sum_hbm,
    b_mid_ref,
    out_hbm,
    w_mid_ref,
    spread_ref,
    picked_ref,
    placed_ref,
    edge_ref,
    input_ref,
    active_ref,
    mixed_ref,
    hidden_ref,
    sums_ref,
    mix_ref,
    out_ref,
    w_sem,
    out_sem,
):
    def fetch(k, r):
        source, t = ((w_mid_hbm, 0), (w_sum_hbm, 0), (w_sum_hbm, 1), (w_mid_hbm, 2))[k]
        return pltpu.make_async_copy(source.at[t, r], w_mid_ref.at[k, r], w_sem.at[k, r])

    def start_rows(k):
        def body(r, carry):
            fetch(k, r).start()
            return carry

        lax.fori_loop(0, 3, body, 0)

    def wait_rows(k):
        for r in range(3):
            fetch(k, r).wait()

    for k in (1, 0, 2, 3):
        start_rows(k)
    chips = devices // GROUP
    c_mid = gain_ref.shape[0]
    tile = lax.rem(lax.axis_index("sp") + OFFSET, devices)
    band = lax.rem(tile, HBANDS)
    time_block = lax.div(tile, HBANDS)
    token_rows = HALF_ROWS + 2
    wide = (HB + 2) * HALF_W
    tall = HB * HALF_W

    blank = jnp.zeros((C_LAT, c_mid), BF16)
    for tap in range(3):
        for tap_row in range(4):
            for spot in range(4):
                at = slice(tap_row * PATCH + spot * C_LAT, tap_row * PATCH + (spot + 1) * C_LAT)
                even = w_in_ref[tap, tap_row, spot] if tap_row < 3 and spot < 3 else blank
                odd = w_in_ref[tap, tap_row, spot - 1] if tap_row < 3 and spot > 0 else blank
                spread_ref[tap, at, :c_mid] = even
                spread_ref[tap, at, c_mid:] = odd

    k = lax.broadcasted_iota(jnp.int32, (256, 256), 0)
    lane = lax.broadcasted_iota(jnp.int32, (256, 256), 1)
    within = lane & 63
    swap = ((lane >> 6) ^ (lane >> 7)) & 1
    source = swap * (2 * C_LAT) + jnp.where(
        within < C_LAT,
        within + C_LAT,
        jnp.where(within < 3 * C_LAT, within - C_LAT, within - 3 * C_LAT),
    )
    layout = jnp.where((k == source) | (k == source + 128 + PATCH), 1.0, 0.0).astype(BF16)

    def arrivals(pieces):
        codes, tokens = {}, {}
        for high, start, stop in pieces:
            code_row = rows - 2 + high
            codes[high] = jnp.concatenate(
                [
                    arrived_ref[s * rows + code_row : s * rows + code_row + 1, start:stop]
                    for s in range(chips)
                ],
                1,
            ).astype(F32)
            if stop - start == rows:
                parts = [arrived_ref[...]]
            else:
                parts = [
                    arrived_ref[s * rows + start : s * rows + stop, :]
                    for s in range(chips)
                ]
            tokens[high] = jnp.concatenate(parts, 0)
        return codes, tokens

    by_age = [arrivals(slot_pieces(0, own_slots, half, rows))]
    if blocks > 1:
        by_age.append(arrivals(slot_pieces(slots - old_slots, slots, half, rows)))

    column = lax.broadcasted_iota(jnp.int32, (HALF_W, 1), 0)
    lanes = lax.broadcasted_iota(jnp.int32, (1, 1, 256), 2) & 63
    from_left, from_right = lanes < C_LAT, lanes >= 3 * C_LAT
    upper = lax.broadcasted_iota(jnp.int32, (1, 1, 128), 2) < PATCH

    def picks(f):
        if f < 0:
            return []
        frame = (time_block - (blocks - 1)) * TB + f
        codes, tokens = by_age[0 if f >= TB * (blocks - 1) else 1]

        def pick(start, stop):
            def step():
                picked = {}
                for high in codes:
                    picks = []
                    for i in range(start, stop):
                        token_row = band * HALF_ROWS - 1 + i
                        valid = (
                            (frame >= 0) & (token_row >= 0) & (token_row < HALF_ROWS * HBANDS)
                        )
                        frame_in = lax.max(frame, 0)
                        row_in = lax.max(token_row, 0)
                        base = (
                            lax.rem(lax.div(frame_in, TB), 3) * 3
                            + lax.rem(lax.div(row_in, HALF_ROWS), 3)
                        ) * TILE_TOKENS + (
                            lax.rem(frame_in, TB) * HALF_ROWS + lax.rem(row_in, HALF_ROWS)
                        ) * HALF_W
                        code = jnp.where(valid, place_code(base + column), -1).astype(F32)
                        picks.append(jnp.where(codes[high] == code, 1.0, 0.0).astype(BF16))
                    picked[high] = jnp.dot(
                        jnp.concatenate(picks, 0), tokens[high], preferred_element_type=F32
                    ).astype(BF16)
                    picked_ref[f, start * HALF_W : stop * HALF_W, high * 128 : high * 128 + 128] = (
                        picked[high]
                    )
                for high in range(2):
                    if high not in codes:
                        picked_ref[
                            f, start * HALF_W : stop * HALF_W, high * 128 : high * 128 + 128
                        ] = jnp.zeros(((stop - start) * HALF_W, 128), BF16)

            return step

        return [pick(0, token_rows // 2), pick(token_rows // 2, token_rows)]

    def edges(f):
        if f < 0:
            return []

        def spread():
            placed_ref[f] = jnp.dot(picked_ref[f], layout, preferred_element_type=F32)

        def shift():
            placed = placed_ref[f].reshape(token_rows, HALF_W, 256)
            gap = jnp.zeros((token_rows, 1, 256), F32)
            left = jnp.concatenate([gap, placed[:, :-1]], 1)
            right = jnp.concatenate([placed[:, 1:], gap], 1)
            placed = jnp.where(from_left, left, jnp.where(from_right, right, placed))
            even_rows, odd_rows = placed[:, :, :128], placed[:, :, 128:]
            below = jnp.concatenate([odd_rows[1:], jnp.zeros((1, HALF_W, 128), F32)], 0)
            odd_rows = jnp.where(upper, odd_rows, below)
            for i in range(token_rows):
                start = 2 * i * HALF_W
                edge_ref[f, start : start + HALF_W, :] = even_rows[i].astype(BF16)
                edge_ref[f, start + HALF_W : start + 2 * HALF_W, :] = odd_rows[i].astype(BF16)

        return [spread, shift]

    index = lax.broadcasted_iota(jnp.int32, (HALF_W, 1), 0)
    bias = b_in_ref[...].reshape(1, c_mid)
    gain = gain_ref[...].reshape(1, c_mid)
    bias_mid = b_mid_ref[...].reshape(1, c_mid)

    def convolved(a):
        def convolve(part):
            def step():
                windows, kernels = [], []
                for tap in range(3):
                    f = TB * (blocks - 1) - 4 + a + tap
                    if f < 0:
                        continue
                    windows += [
                        edge_ref[f, 0:wide, :],
                        edge_ref[f, 2 * HALF_W : 2 * HALF_W + wide, :],
                    ]
                    kernels.append(spread_ref[tap, :, part])
                input_ref[a, :, part] = jnp.dot(
                    jnp.concatenate(windows, 1),
                    jnp.concatenate(kernels, 0),
                    preferred_element_type=F32,
                )

            return step

        return [convolve(slice(n, n + 256)) for n in range(0, 2 * c_mid, 256)]

    def activated(a):
        def normalise(r, p):
            def step():
                part = slice(p * c_mid, (p + 1) * c_mid)
                at = slice(r * HALF_W, (r + 1) * HALF_W)
                hidden = (input_ref[a, at, part] + bias).astype(BF16)
                if a >= 2 and 1 <= r <= HB:
                    hidden_ref[a - 2, (r - 1) * HALF_W : r * HALF_W, part] = hidden
                values = hidden.astype(F32)
                mean = jnp.sum(values * values, 1, keepdims=True) * (1.0 / c_mid)
                inverse = lax.rsqrt(mean + 1e-06) * 0.5
                keep = time_block * TB - 2 + a >= 0
                if r in (0, HB + 1):
                    row = band * HB - 1 + r
                    keep = keep & (row >= 0) & (row < HB * HBANDS)
                halved = values * jnp.where(keep, inverse, 0.0) * gain
                active_ref[a, at, part] = (halved + halved * jnp.tanh(halved)).astype(BF16)

            return step

        return [normalise(r, p) for r in range(HB + 2) for p in range(2)]

    halves = 2
    part_rows = tall // halves

    def mix(k):
        def rows_of(start):
            def step():
                at = slice(start, start + 2 * HALF_W)
                one, two, sign = ((0, 2, -1), (1, 2, 1), (2, 1, -1), (1, 3, -1))[k]
                first, second = active_ref[one, at, :], active_ref[two, at, :]
                mixed_ref[k, at, :] = first + second if sign > 0 else first - second

            return step

        return [rows_of(start) for start in range(0, wide, 2 * HALF_W)]

    def product(k, h):
        def piece(source, part, kernel):
            def step():
                windows = [
                    mixed_ref[k, r * HALF_W + h * part_rows : r * HALF_W + (h + 1) * part_rows, source]
                    for r in range(3)
                ]
                value = jnp.dot(
                    jnp.concatenate(windows, 1), kernel(), preferred_element_type=F32
                )
                at = slice(h * part_rows, (h + 1) * part_rows)
                if k == 1:
                    sums_ref[1, at, part] = value
                elif k == 0:
                    sums_ref[0, at, part] = sums_ref[1, at, part] + value
                elif k == 2:
                    sums_ref[0, at, part] = sums_ref[0, at, part] + value
                    sums_ref[1, at, part] = sums_ref[1, at, part] - value
                else:
                    sums_ref[1, at, part] = sums_ref[1, at, part] - value

            return step

        def taps(column_tap, start, stop):
            return [w_mid_ref[k, r, column_tap, :, start:stop] for r in range(3)]

        def straight(start, stop):
            def kernel():
                blocks_of = []
                for r in range(3):
                    for even_tap, odd_tap in ((1, 0), (2, 1)):
                        columns = []
                        if start < c_mid:
                            columns.append(
                                w_mid_ref[k, r, even_tap, :, start : min(stop, c_mid)]
                            )
                        if stop > c_mid:
                            columns.append(
                                w_mid_ref[k, r, odd_tap, :, max(start, c_mid) - c_mid : stop - c_mid]
                            )
                        blocks_of.append(
                            columns[0] if len(columns) == 1 else jnp.concatenate(columns, 1)
                        )
                return jnp.concatenate(blocks_of, 0)

            return kernel

        def side(column_tap, start, stop):
            return lambda: jnp.concatenate(taps(column_tap, start, stop), 0)

        def both_sides(start):
            def kernel():
                width = c_mid - start
                gap = jnp.zeros((c_mid, width), BF16)
                blocks_of = []
                for right, left in zip(taps(2, start, c_mid), taps(0, start, c_mid)):
                    blocks_of.append(jnp.concatenate([right, gap], 1))
                    blocks_of.append(jnp.concatenate([gap, left], 1))
                return jnp.concatenate(blocks_of, 0)

            return kernel

        whole = slice(0, 2 * c_mid)
        straights = [
            piece(whole, slice(n, n + 256), straight(n, n + 256)) for n in range(0, 2 * c_mid, 256)
        ]
        full = c_mid // 256 * 256
        sides = [
            piece(slice(0, c_mid), slice(2 * c_mid, 2 * c_mid + full), side(2, 0, full)),
            piece(
                slice(c_mid, 2 * c_mid), slice(2 * c_mid + full, 2 * c_mid + 2 * full), side(0, 0, full)
            ),
            piece(whole, slice(2 * c_mid + 2 * full, 4 * c_mid), both_sides(full)),
        ]
        return straights[:2] + sides[:2] + straights[2:] + sides[2:]

    full = c_mid // 256 * 256
    rest = c_mid - full

    def finish(o, h):
        out_rows = 2 * part_rows

        def lane_group(g):
            def step():
                at = slice(h * part_rows, (h + 1) * part_rows)
                lanes_of = slice(g * 128, (g + 1) * 128)

                def columns(start):
                    return sums_ref[o, at, start : start + 128]

                if g * 128 < full:
                    right = 2 * c_mid + g * 128
                    left = right + full
                else:
                    right = 2 * c_mid + 2 * full + g * 128 - full
                    left = right + rest
                gap = jnp.zeros((HB // halves, 1, 128), F32)
                shape = (HB // halves, HALF_W, 128)
                to_odd = jnp.concatenate([columns(right).reshape(shape)[:, 1:], gap], 1)
                to_even = jnp.concatenate([gap, columns(left).reshape(shape)[:, :-1]], 1)
                for p, moved in ((0, to_even), (1, to_odd)):
                    start = p * c_mid + g * 128
                    hidden = hidden_ref[o, at, start : start + 128].astype(F32)
                    mix_ref[o, h, g, pl.ds(p, part_rows, stride=2), :] = (
                        columns(start)
                        + moved.reshape(part_rows, 128)
                        + bias_mid[:, lanes_of]
                        + hidden
                    )
                out_ref[o, h * out_rows : (h + 1) * out_rows, lanes_of] = mix_ref[o, h, g].astype(
                    BF16
                )
                leave(o, h, g).start()

            return step

        return [lane_group(g) for g in range(c_mid // 128)]

    def leave(o, h, g):
        out_rows = 2 * part_rows
        lanes_of = pl.ds(g * 128, 128)
        return pltpu.make_async_copy(
            out_ref.at[o, pl.ds(h * out_rows, out_rows), lanes_of],
            out_hbm.at[pl.ds(o * 2 * tall + h * out_rows, out_rows), lanes_of],
            out_sem.at[o, h, g],
        )

    newest = TB * (blocks - 1) - 2
    for f in range(newest):
        run(picks(f) + edges(f))
    run(picks(newest) + picks(newest + 1))
    run(edges(newest), picks(newest + 2))
    run(edges(newest + 1) + convolved(1), picks(newest + 3))
    run(edges(newest + 2) + convolved(2), activated(1))
    run(edges(newest + 3) + convolved(0) + convolved(3), activated(2))
    for k in range(4):
        wait_rows(k)
    run(mix(1))
    run(product(1, 0) + product(1, 1), activated(0) + mix(0))
    run(product(0, 0) + product(0, 1), mix(2))
    run(product(2, 0) + product(2, 1), activated(3) + mix(3))
    run(product(3, 0), finish(0, 0) + finish(0, 1))
    last = finish(1, 1)
    run(product(3, 1)[:4], finish(1, 0))
    run(last[:1] + product(3, 1)[4:5] + last[1:2] + product(3, 1)[5:] + last[2:])
    for o in range(TB):
        for h in range(halves):
            for g in range(c_mid // 128):
                leave(o, h, g).wait()


def shards(latents, row_cell, w_in, b_in, gain, w_mid, b_mid):
    devices = lax.axis_size("sp")
    tokens = latents.shape[0]
    c_mid = gain.shape[0]
    blocks = min(3, devices // HBANDS)
    chips = devices // GROUP
    pair = tokens // devices
    bands = GROUP + 2
    own_slots = pair * bands + pair
    old_slots = pair * bands * (blocks - 1) + pair
    slots = pair * bands * blocks + pair
    half = -(-slots // 2)
    rows = -(-(half + 2) // 8) * 8
    outgoing = pl.pallas_call(
        functools.partial(pack_kernel, devices, rows, half, slots),
        out_shape=jax.ShapeDtypeStruct((chips * rows, 128), BF16),
        in_specs=[VMEM, VMEM],
        out_specs=VMEM,
        name="pack",
    )(row_cell, latents.T)
    arrived = lax.all_to_all(
        outgoing.reshape(chips, rows, 128), "sp", split_axis=0, concat_axis=0, tiled=True
    )
    w_sum = pl.pallas_call(
        weight_kernel,
        grid=(3, 3),
        out_shape=jax.ShapeDtypeStruct((2, 3, 3, c_mid, c_mid), BF16),
        in_specs=[pl.BlockSpec((3, 1, 1, c_mid, c_mid), lambda i, j: (0, i, j, 0, 0))],
        out_specs=pl.BlockSpec((2, 1, 1, c_mid, c_mid), lambda i, j: (0, i, j, 0, 0)),
        name="weights",
    )(w_mid)
    wide = (HB + 2) * HALF_W
    tall = HB * HALF_W
    frames = TB * blocks
    decoded = pl.pallas_call(
        functools.partial(
            main_kernel, devices, blocks, rows, half, own_slots, old_slots, slots
        ),
        out_shape=jax.ShapeDtypeStruct((TB * HB * W, c_mid), BF16),
        in_specs=[VMEM, VMEM, VMEM, VMEM, HBM, HBM, VMEM],
        out_specs=HBM,
        scratch_shapes=[
            pltpu.VMEM((4, 3, 3, c_mid, c_mid), BF16),
            pltpu.VMEM((3, 4 * PATCH, 2 * c_mid), BF16),
            pltpu.VMEM((frames, (HALF_ROWS + 2) * HALF_W, 256), BF16),
            pltpu.VMEM((frames, (HALF_ROWS + 2) * HALF_W, 256), F32),
            pltpu.VMEM((frames, 2 * (HALF_ROWS + 2) * HALF_W, 128), BF16),
            pltpu.VMEM((TB + 2, wide, 2 * c_mid), F32),
            pltpu.VMEM((TB + 2, wide, 2 * c_mid), BF16),
            pltpu.VMEM((4, wide, 2 * c_mid), BF16),
            pltpu.VMEM((TB, tall, 2 * c_mid), BF16),
            pltpu.VMEM((2, tall, 4 * c_mid), F32),
            pltpu.VMEM((TB, 2, c_mid // 128, tall, 128), F32),
            pltpu.VMEM((TB, 2 * tall, c_mid), BF16),
            pltpu.SemaphoreType.DMA((4, 3)),
            pltpu.SemaphoreType.DMA((TB, 2, c_mid // 128)),
        ],
        compiler_params=pltpu.CompilerParams(vmem_limit_bytes=48 * 1024 * 1024),
        name="block",
    )(
        arrived.reshape(chips * rows, 128),
        w_in,
        b_in,
        gain,
        w_mid,
        pltpu.with_memory_space_constraint(w_sum, pltpu.HBM),
        b_mid,
    )
    return decoded.reshape(1, TB, HB, W, c_mid)


def solution(mesh):
    return jax.shard_map(
        shards,
        mesh=mesh,
        in_specs=(P(("grp", "sp"), None), P(("grp", "sp")), P(), P(), P(), P(), P()),
        out_specs=P(("grp", "sp"), None, None, None, None),
        check_vma=False,
    )
```

```python
import functools

import jax
import jax.numpy as jnp
from jax import lax
from jax.experimental import pallas as pl
from jax.experimental.pallas import tpu as pltpu
from jax.sharding import PartitionSpec as P

C_LAT = 16
W = 160
TB = 2
HBANDS = 8
HB = 4
OFFSET = 2 * HBANDS + HBANDS // 2
HALF_ROWS = HB // 2
HALF_W = W // 2
TILE_TOKENS = TB * HALF_ROWS * HALF_W
PATCH = 4 * C_LAT
GROUP = 1
F32 = jnp.float32
BF16 = jnp.bfloat16
VMEM = pl.BlockSpec(memory_space=pltpu.VMEM)
HBM = pl.BlockSpec(memory_space=pltpu.HBM)


def place_code(index):
    return ((index & 127) + 128) << (index >> 7)


def select(picks, values):
    return lax.dot_general(picks, values, (((1,), (1,)), ((), ())), preferred_element_type=F32)


def pack_kernel(devices, rows, half, slots, cells_ref, latents_ref, out_ref):
    chips = devices // GROUP
    count = latents_ref.shape[1]
    tokens = -(-count // 128) * 128
    cells = cells_ref[...].reshape(1, count)
    latents = latents_ref[...]
    if tokens > count:
        cells = jnp.concatenate([cells, jnp.full((1, tokens - count), 1 << 20, jnp.int32)], 1)
        latents = jnp.concatenate(
            [latents, jnp.zeros((latents.shape[0], tokens - count), latents.dtype)], 1
        )
    column = lax.rem(cells, HALF_W)
    token_row = lax.rem(lax.div(cells, HALF_W), HALF_ROWS * HBANDS)
    frame = lax.div(cells, HALF_W * HALF_ROWS * HBANDS)
    block = lax.div(frame, TB)
    band = lax.div(token_row, HALF_ROWS)
    side = lax.rem(token_row, HALF_ROWS)
    local = (lax.rem(frame, TB) * HALF_ROWS + side) * HALF_W + column
    code = place_code((lax.rem(block, 3) * 3 + lax.rem(band, 3)) * TILE_TOKENS + local)
    code = code.astype(F32)

    chip = lax.broadcasted_iota(jnp.int32, (chips, tokens), 0)
    tile = lax.rem(chip * GROUP + OFFSET, devices)
    top = lax.rem(tile, HBANDS)
    bottom = top + GROUP - 1
    age = lax.div(tile, HBANDS) - block
    near = (
        ((band >= top) & (band <= bottom))
        | ((band == top - 1) & (side == HALF_ROWS - 1))
        | ((band == bottom + 1) & (side == 0))
    )
    own = jnp.where(near & (age == 0), 1.0, 0.0)
    old = jnp.where(near & (age > 0) & (age < 3), 1.0, 0.0)
    before = lax.broadcasted_iota(jnp.int32, (tokens, tokens), 0) < lax.broadcasted_iota(
        jnp.int32, (tokens, tokens), 1
    )
    before = jnp.where(before, 1.0, 0.0).astype(BF16)
    ranks = jnp.dot(
        jnp.concatenate([own, old], 0).astype(BF16), before, preferred_element_type=F32
    )
    rank = jnp.where(
        own > 0.5, ranks[:chips], jnp.where(old > 0.5, slots - 1 - ranks[chips:], -1.0)
    )

    slot = lax.broadcasted_iota(jnp.int32, (rows, tokens), 0).astype(F32)
    low_slot = jnp.where(slot < half, slot, -7.0)
    high_slot = jnp.where(slot < half, slot + half, -7.0)
    blank = jnp.zeros_like(latents)
    codes = jnp.broadcast_to(code, (128, tokens)).astype(BF16)
    low_values = jnp.concatenate([latents, blank, codes], 0)
    high_values = jnp.concatenate([blank, latents, codes], 0)
    low_out = select(
        jnp.concatenate(
            [jnp.where(rank[d : d + 1] == low_slot, 1.0, 0.0).astype(BF16) for d in range(chips)], 0
        ),
        low_values,
    )
    high_out = select(
        jnp.concatenate(
            [jnp.where(rank[d : d + 1] == high_slot, 1.0, 0.0).astype(BF16) for d in range(chips)],
            0,
        ),
        high_values,
    )
    row = lax.broadcasted_iota(jnp.int32, (rows, 128), 0)
    diagonal = row == lax.broadcasted_iota(jnp.int32, (rows, 128), 1)
    for d in range(chips):
        part = slice(d * rows, (d + 1) * rows)
        low_codes = jnp.sum(jnp.where(diagonal, low_out[part, 128:], 0.0), 0, keepdims=True)
        high_codes = jnp.sum(jnp.where(diagonal, high_out[part, 128:], 0.0), 0, keepdims=True)
        body = low_out[part, :128] + high_out[part, :128]
        body = jnp.where(row == rows - 2, low_codes, body)
        body = jnp.where(row == rows - 1, high_codes, body)
        out_ref[part, :] = body.astype(BF16)


def weight_kernel(w_ref, sums_ref):
    first, middle, last = (w_ref[t].astype(F32) * 0.5 for t in range(3))
    outer = first + last
    sums_ref[0] = (outer + middle).astype(BF16)
    sums_ref[1] = (outer - middle).astype(BF16)


def slot_pieces(first, last, half, rows):
    pieces = []
    for high, start, stop in (
        (0, first, min(last, half)),
        (1, max(first, half) - half, last - half),
    ):
        if start < stop:
            pieces.append((high, start // 8 * 8, min(rows, -(-stop // 8) * 8)))
    return pieces


def run(*lists):
    steps = []
    for which, steps_of in enumerate(lists):
        for i, step in enumerate(steps_of):
            steps.append(((i + 0.5) / len(steps_of), which, i, step))
    for step in sorted(steps, key=lambda entry: entry[:3]):
        step[3]()


def main_kernel(
    devices,
    blocks,
    rows,
    half,
    own_slots,
    old_slots,
    slots,
    arrived_ref,
    w_in_ref,
    b_in_ref,
    gain_ref,
    w_mid_hbm,
    w_sum_hbm,
    b_mid_ref,
    out_hbm,
    w_mid_ref,
    spread_ref,
    picked_ref,
    placed_ref,
    edge_ref,
    input_ref,
    active_ref,
    mixed_ref,
    hidden_ref,
    sums_ref,
    mix_ref,
    out_ref,
    w_sem,
    out_sem,
):
    def fetch(k, r):
        source, t = ((w_mid_hbm, 0), (w_sum_hbm, 0), (w_sum_hbm, 1), (w_mid_hbm, 2))[k]
        return pltpu.make_async_copy(source.at[t, r], w_mid_ref.at[k, r], w_sem.at[k, r])

    def start_rows(k):
        def body(r, carry):
            fetch(k, r).start()
            return carry

        lax.fori_loop(0, 3, body, 0)

    def wait_rows(k):
        for r in range(3):
            fetch(k, r).wait()

    for k in (1, 0, 2, 3):
        start_rows(k)
    chips = devices // GROUP
    c_mid = gain_ref.shape[0]
    tile = lax.rem(lax.axis_index("sp") + OFFSET, devices)
    band = lax.rem(tile, HBANDS)
    time_block = lax.div(tile, HBANDS)
    token_rows = HALF_ROWS + 2
    wide = (HB + 2) * HALF_W
    tall = HB * HALF_W

    blank = jnp.zeros((C_LAT, c_mid), BF16)
    for tap in range(3):
        for tap_row in range(4):
            for spot in range(4):
                at = slice(tap_row * PATCH + spot * C_LAT, tap_row * PATCH + (spot + 1) * C_LAT)
                even = w_in_ref[tap, tap_row, spot] if tap_row < 3 and spot < 3 else blank
                odd = w_in_ref[tap, tap_row, spot - 1] if tap_row < 3 and spot > 0 else blank
                spread_ref[tap, at, :c_mid] = even
                spread_ref[tap, at, c_mid:] = odd

    k = lax.broadcasted_iota(jnp.int32, (256, 256), 0)
    lane = lax.broadcasted_iota(jnp.int32, (256, 256), 1)
    within = lane & 63
    swap = ((lane >> 6) ^ (lane >> 7)) & 1
    source = swap * (2 * C_LAT) + jnp.where(
        within < C_LAT,
        within + C_LAT,
        jnp.where(within < 3 * C_LAT, within - C_LAT, within - 3 * C_LAT),
    )
    layout = jnp.where((k == source) | (k == source + 128 + PATCH), 1.0, 0.0).astype(BF16)

    def arrivals(pieces):
        codes, tokens = {}, {}
        for high, start, stop in pieces:
            code_row = rows - 2 + high
            codes[high] = jnp.concatenate(
                [
                    arrived_ref[s * rows + code_row : s * rows + code_row + 1, start:stop]
                    for s in range(chips)
                ],
                1,
            )
            if stop - start == rows:
                parts = [arrived_ref[...]]
            else:
                parts = [
                    arrived_ref[s * rows + start : s * rows + stop, :]
                    for s in range(chips)
                ]
            tokens[high] = jnp.concatenate(parts, 0)
        return codes, tokens

    by_age = [arrivals(slot_pieces(0, own_slots, half, rows))]
    if blocks > 1:
        by_age.append(arrivals(slot_pieces(slots - old_slots, slots, half, rows)))

    one, zero = jnp.ones((), BF16), jnp.zeros((), BF16)
    column = lax.broadcasted_iota(jnp.int32, (HALF_W, 1), 0)
    lanes = lax.broadcasted_iota(jnp.int32, (1, 1, 256), 2) & 63
    from_left, from_right = lanes < C_LAT, lanes >= 3 * C_LAT
    upper = lax.broadcasted_iota(jnp.int32, (1, 1, 128), 2) < PATCH

    def picks(f):
        if f < 0:
            return []
        frame = (time_block - (blocks - 1)) * TB + f
        codes, tokens = by_age[0 if f >= TB * (blocks - 1) else 1]

        def pick(start, stop):
            def step():
                picked = {}
                for high in codes:
                    picks = []
                    for i in range(start, stop):
                        token_row = band * HALF_ROWS - 1 + i
                        valid = (
                            (frame >= 0) & (token_row >= 0) & (token_row < HALF_ROWS * HBANDS)
                        )
                        frame_in = lax.max(frame, 0)
                        row_in = lax.max(token_row, 0)
                        base = (
                            lax.rem(lax.div(frame_in, TB), 3) * 3
                            + lax.rem(lax.div(row_in, HALF_ROWS), 3)
                        ) * TILE_TOKENS + (
                            lax.rem(frame_in, TB) * HALF_ROWS + lax.rem(row_in, HALF_ROWS)
                        ) * HALF_W
                        code = jnp.where(valid, place_code(base + column), -1).astype(F32).astype(BF16)
                        picks.append(jnp.where(codes[high] == code, one, zero))
                    picked[high] = jnp.dot(
                        jnp.concatenate(picks, 0), tokens[high], preferred_element_type=F32
                    ).astype(BF16)
                    picked_ref[f, start * HALF_W : stop * HALF_W, high * 128 : high * 128 + 128] = (
                        picked[high]
                    )
                for high in range(2):
                    if high not in codes:
                        picked_ref[
                            f, start * HALF_W : stop * HALF_W, high * 128 : high * 128 + 128
                        ] = jnp.zeros(((stop - start) * HALF_W, 128), BF16)

            return step

        return [pick(0, token_rows // 2), pick(token_rows // 2, token_rows)]

    def edges(f):
        if f < 0:
            return []

        def spread():
            placed_ref[f] = jnp.dot(picked_ref[f], layout, preferred_element_type=F32)

        def shift():
            placed = placed_ref[f].reshape(token_rows, HALF_W, 256)
            gap = jnp.zeros((token_rows, 1, 256), F32)
            left = jnp.concatenate([gap, placed[:, :-1]], 1)
            right = jnp.concatenate([placed[:, 1:], gap], 1)
            placed = jnp.where(from_left, left, jnp.where(from_right, right, placed))
            even_rows, odd_rows = placed[:, :, :128], placed[:, :, 128:]
            below = jnp.concatenate([odd_rows[1:], jnp.zeros((1, HALF_W, 128), F32)], 0)
            odd_rows = jnp.where(upper, odd_rows, below)
            for i in range(token_rows):
                start = 2 * i * HALF_W
                edge_ref[f, start : start + HALF_W, :] = even_rows[i].astype(BF16)
                edge_ref[f, start + HALF_W : start + 2 * HALF_W, :] = odd_rows[i].astype(BF16)

        return [spread, shift]

    index = lax.broadcasted_iota(jnp.int32, (HALF_W, 1), 0)
    bias = b_in_ref[...].reshape(1, c_mid)
    gain = gain_ref[...].reshape(1, c_mid)
    bias_mid = b_mid_ref[...].reshape(1, c_mid)

    def convolved(a):
        def convolve(part):
            def step():
                windows, kernels = [], []
                for tap in range(3):
                    f = TB * (blocks - 1) - 4 + a + tap
                    if f < 0:
                        continue
                    windows += [
                        edge_ref[f, 0:wide, :],
                        edge_ref[f, 2 * HALF_W : 2 * HALF_W + wide, :],
                    ]
                    kernels.append(spread_ref[tap, :, part])
                input_ref[a, :, part] = jnp.dot(
                    jnp.concatenate(windows, 1),
                    jnp.concatenate(kernels, 0),
                    preferred_element_type=F32,
                )

            return step

        return [convolve(slice(n, n + 256)) for n in range(0, 2 * c_mid, 256)]

    def activated(a):
        def normalise(r, p):
            def step():
                part = slice(p * c_mid, (p + 1) * c_mid)
                at = slice(r * HALF_W, (r + 1) * HALF_W)
                hidden = (input_ref[a, at, part] + bias).astype(BF16)
                if a >= 2 and 1 <= r <= HB:
                    hidden_ref[a - 2, (r - 1) * HALF_W : r * HALF_W, part] = hidden
                values = hidden.astype(F32)
                mean = jnp.sum(values * values, 1, keepdims=True) * (1.0 / c_mid)
                inverse = lax.rsqrt(mean + 1e-06) * 0.5
                keep = time_block * TB - 2 + a >= 0
                if r in (0, HB + 1):
                    row = band * HB - 1 + r
                    keep = keep & (row >= 0) & (row < HB * HBANDS)
                halved = values * jnp.where(keep, inverse, 0.0) * gain
                active_ref[a, at, part] = (halved + halved * jnp.tanh(halved)).astype(BF16)

            return step

        return [normalise(r, p) for r in range(HB + 2) for p in range(2)]

    halves = 2
    part_rows = tall // halves

    def mix(k):
        def rows_of(start):
            def step():
                at = slice(start, start + 2 * HALF_W)
                one, two, sign = ((0, 2, -1), (1, 2, 1), (2, 1, -1), (1, 3, -1))[k]
                first, second = active_ref[one, at, :], active_ref[two, at, :]
                mixed_ref[k, at, :] = first + second if sign > 0 else first - second

            return step

        return [rows_of(start) for start in range(0, wide, 2 * HALF_W)]

    def product(k, h):
        def piece(source, part, kernel):
            def step():
                windows = [
                    mixed_ref[k, r * HALF_W + h * part_rows : r * HALF_W + (h + 1) * part_rows, source]
                    for r in range(3)
                ]
                value = jnp.dot(
                    jnp.concatenate(windows, 1), kernel(), preferred_element_type=F32
                )
                at = slice(h * part_rows, (h + 1) * part_rows)
                if k == 1:
                    sums_ref[1, at, part] = value
                elif k == 0:
                    sums_ref[0, at, part] = sums_ref[1, at, part] + value
                elif k == 2:
                    sums_ref[0, at, part] = sums_ref[0, at, part] + value
                    sums_ref[1, at, part] = sums_ref[1, at, part] - value
                else:
                    sums_ref[1, at, part] = sums_ref[1, at, part] - value

            return step

        def taps(column_tap, start, stop):
            return [w_mid_ref[k, r, column_tap, :, start:stop] for r in range(3)]

        def straight(start, stop):
            def kernel():
                blocks_of = []
                for r in range(3):
                    for even_tap, odd_tap in ((1, 0), (2, 1)):
                        columns = []
                        if start < c_mid:
                            columns.append(
                                w_mid_ref[k, r, even_tap, :, start : min(stop, c_mid)]
                            )
                        if stop > c_mid:
                            columns.append(
                                w_mid_ref[k, r, odd_tap, :, max(start, c_mid) - c_mid : stop - c_mid]
                            )
                        blocks_of.append(
                            columns[0] if len(columns) == 1 else jnp.concatenate(columns, 1)
                        )
                return jnp.concatenate(blocks_of, 0)

            return kernel

        def side(column_tap, start, stop):
            return lambda: jnp.concatenate(taps(column_tap, start, stop), 0)

        def both_sides(start):
            def kernel():
                width = c_mid - start
                gap = jnp.zeros((c_mid, width), BF16)
                blocks_of = []
                for right, left in zip(taps(2, start, c_mid), taps(0, start, c_mid)):
                    blocks_of.append(jnp.concatenate([right, gap], 1))
                    blocks_of.append(jnp.concatenate([gap, left], 1))
                return jnp.concatenate(blocks_of, 0)

            return kernel

        whole = slice(0, 2 * c_mid)
        straights = [
            piece(whole, slice(n, n + 256), straight(n, n + 256)) for n in range(0, 2 * c_mid, 256)
        ]
        full = c_mid // 256 * 256
        sides = [
            piece(slice(0, c_mid), slice(2 * c_mid, 2 * c_mid + full), side(2, 0, full)),
            piece(
                slice(c_mid, 2 * c_mid), slice(2 * c_mid + full, 2 * c_mid + 2 * full), side(0, 0, full)
            ),
            piece(whole, slice(2 * c_mid + 2 * full, 4 * c_mid), both_sides(full)),
        ]
        return straights[:2] + sides[:2] + straights[2:] + sides[2:]

    full = c_mid // 256 * 256
    rest = c_mid - full

    def finish(o, h):
        out_rows = 2 * part_rows

        def lane_group(g):
            def step():
                at = slice(h * part_rows, (h + 1) * part_rows)
                lanes_of = slice(g * 128, (g + 1) * 128)

                def columns(start):
                    return sums_ref[o, at, start : start + 128]

                if g * 128 < full:
                    right = 2 * c_mid + g * 128
                    left = right + full
                else:
                    right = 2 * c_mid + 2 * full + g * 128 - full
                    left = right + rest
                gap = jnp.zeros((HB // halves, 1, 128), F32)
                shape = (HB // halves, HALF_W, 128)
                to_odd = jnp.concatenate([columns(right).reshape(shape)[:, 1:], gap], 1)
                to_even = jnp.concatenate([gap, columns(left).reshape(shape)[:, :-1]], 1)
                for p, moved in ((0, to_even), (1, to_odd)):
                    start = p * c_mid + g * 128
                    hidden = hidden_ref[o, at, start : start + 128].astype(F32)
                    mix_ref[o, h, g, pl.ds(p, part_rows, stride=2), :] = (
                        columns(start)
                        + moved.reshape(part_rows, 128)
                        + bias_mid[:, lanes_of]
                        + hidden
                    )
                out_ref[o, h * out_rows : (h + 1) * out_rows, lanes_of] = mix_ref[o, h, g].astype(
                    BF16
                )
                leave(o, h, g).start()

            return step

        return [lane_group(g) for g in range(c_mid // 128)]

    def leave(o, h, g):
        out_rows = 2 * part_rows
        lanes_of = pl.ds(g * 128, 128)
        return pltpu.make_async_copy(
            out_ref.at[o, pl.ds(h * out_rows, out_rows), lanes_of],
            out_hbm.at[pl.ds(o * 2 * tall + h * out_rows, out_rows), lanes_of],
            out_sem.at[o, h, g],
        )

    newest = TB * (blocks - 1) - 2
    for f in range(newest):
        run(picks(f) + edges(f))
    run(picks(newest) + picks(newest + 1))
    run(edges(newest), picks(newest + 2))
    run(edges(newest + 1) + convolved(1), picks(newest + 3))
    run(edges(newest + 2) + convolved(2), activated(1))
    run(edges(newest + 3) + convolved(0) + convolved(3), activated(2))
    for k in range(4):
        wait_rows(k)
    run(mix(1))
    run(product(1, 0) + product(1, 1), activated(0) + mix(0))
    run(product(0, 0) + product(0, 1), mix(2))
    run(product(2, 0) + product(2, 1), activated(3) + mix(3))
    run(product(3, 0), finish(0, 0) + finish(0, 1))
    last = finish(1, 1)
    run(product(3, 1)[:4], finish(1, 0))
    run(last[:1] + product(3, 1)[4:5] + last[1:2] + product(3, 1)[5:] + last[2:])
    for o in range(TB):
        for h in range(halves):
            for g in range(c_mid // 128):
                leave(o, h, g).wait()


def shards(latents, row_cell, w_in, b_in, gain, w_mid, b_mid):
    devices = lax.axis_size("sp")
    tokens = latents.shape[0]
    c_mid = gain.shape[0]
    blocks = min(3, devices // HBANDS)
    chips = devices // GROUP
    pair = tokens // devices
    bands = GROUP + 2
    own_slots = pair * bands + pair
    old_slots = pair * bands * (blocks - 1) + pair
    slots = pair * bands * blocks + pair
    half = -(-slots // 2)
    rows = -(-(half + 2) // 8) * 8
    outgoing = pl.pallas_call(
        functools.partial(pack_kernel, devices, rows, half, slots),
        out_shape=jax.ShapeDtypeStruct((chips * rows, 128), BF16),
        in_specs=[VMEM, VMEM],
        out_specs=VMEM,
        name="pack",
    )(row_cell, latents.T)
    arrived = lax.all_to_all(
        outgoing.reshape(chips, rows, 128), "sp", split_axis=0, concat_axis=0, tiled=True
    )
    w_sum = pl.pallas_call(
        weight_kernel,
        grid=(3, 3),
        out_shape=jax.ShapeDtypeStruct((2, 3, 3, c_mid, c_mid), BF16),
        in_specs=[pl.BlockSpec((3, 1, 1, c_mid, c_mid), lambda i, j: (0, i, j, 0, 0))],
        out_specs=pl.BlockSpec((2, 1, 1, c_mid, c_mid), lambda i, j: (0, i, j, 0, 0)),
        name="weights",
    )(w_mid)
    wide = (HB + 2) * HALF_W
    tall = HB * HALF_W
    frames = TB * blocks
    decoded = pl.pallas_call(
        functools.partial(
            main_kernel, devices, blocks, rows, half, own_slots, old_slots, slots
        ),
        out_shape=jax.ShapeDtypeStruct((TB * HB * W, c_mid), BF16),
        in_specs=[VMEM, VMEM, VMEM, VMEM, HBM, HBM, VMEM],
        out_specs=HBM,
        scratch_shapes=[
            pltpu.VMEM((4, 3, 3, c_mid, c_mid), BF16),
            pltpu.VMEM((3, 4 * PATCH, 2 * c_mid), BF16),
            pltpu.VMEM((frames, (HALF_ROWS + 2) * HALF_W, 256), BF16),
            pltpu.VMEM((frames, (HALF_ROWS + 2) * HALF_W, 256), F32),
            pltpu.VMEM((frames, 2 * (HALF_ROWS + 2) * HALF_W, 128), BF16),
            pltpu.VMEM((TB + 2, wide, 2 * c_mid), F32),
            pltpu.VMEM((TB + 2, wide, 2 * c_mid), BF16),
            pltpu.VMEM((4, wide, 2 * c_mid), BF16),
            pltpu.VMEM((TB, tall, 2 * c_mid), BF16),
            pltpu.VMEM((2, tall, 4 * c_mid), F32),
            pltpu.VMEM((TB, 2, c_mid // 128, tall, 128), F32),
            pltpu.VMEM((TB, 2 * tall, c_mid), BF16),
            pltpu.SemaphoreType.DMA((4, 3)),
            pltpu.SemaphoreType.DMA((TB, 2, c_mid // 128)),
        ],
        compiler_params=pltpu.CompilerParams(vmem_limit_bytes=48 * 1024 * 1024),
        name="block",
    )(
        arrived.reshape(chips * rows, 128),
        w_in,
        b_in,
        gain,
        w_mid,
        pltpu.with_memory_space_constraint(w_sum, pltpu.HBM),
        b_mid,
    )
    return decoded.reshape(1, TB, HB, W, c_mid)


def solution(mesh):
    return jax.shard_map(
        shards,
        mesh=mesh,
        in_specs=(P(("grp", "sp"), None), P(("grp", "sp")), P(), P(), P(), P(), P()),
        out_specs=P(("grp", "sp"), None, None, None, None),
        check_vma=False,
    )
```

```python
import functools

import jax
import jax.numpy as jnp
from jax import lax
from jax.experimental import pallas as pl
from jax.experimental.pallas import tpu as pltpu
from jax.sharding import PartitionSpec as P

C_LAT = 16
W = 160
TB = 2
HBANDS = 8
HB = 4
OFFSET = 2 * HBANDS + HBANDS // 2
HALF_ROWS = HB // 2
HALF_W = W // 2
TILE_TOKENS = TB * HALF_ROWS * HALF_W
PATCH = 4 * C_LAT
GROUP = 1
F32 = jnp.float32
BF16 = jnp.bfloat16
VMEM = pl.BlockSpec(memory_space=pltpu.VMEM)
HBM = pl.BlockSpec(memory_space=pltpu.HBM)


def place_code(index):
    return ((index & 127) + 128) << (index >> 7)


def select(picks, values):
    return lax.dot_general(picks, values, (((1,), (1,)), ((), ())), preferred_element_type=F32)


def pack_kernel(devices, rows, half, slots, cells_ref, latents_ref, out_ref):
    chips = devices // GROUP
    count = latents_ref.shape[1]
    tokens = -(-count // 128) * 128
    cells = cells_ref[...].reshape(1, count)
    latents = latents_ref[...]
    if tokens > count:
        cells = jnp.concatenate([cells, jnp.full((1, tokens - count), 1 << 20, jnp.int32)], 1)
        latents = jnp.concatenate(
            [latents, jnp.zeros((latents.shape[0], tokens - count), latents.dtype)], 1
        )
    column = lax.rem(cells, HALF_W)
    token_row = lax.rem(lax.div(cells, HALF_W), HALF_ROWS * HBANDS)
    frame = lax.div(cells, HALF_W * HALF_ROWS * HBANDS)
    block = lax.div(frame, TB)
    band = lax.div(token_row, HALF_ROWS)
    side = lax.rem(token_row, HALF_ROWS)
    local = (lax.rem(frame, TB) * HALF_ROWS + side) * HALF_W + column
    code = place_code((lax.rem(block, 3) * 3 + lax.rem(band, 3)) * TILE_TOKENS + local)
    code = code.astype(F32)

    chip = lax.broadcasted_iota(jnp.int32, (chips, tokens), 0)
    tile = lax.rem(chip * GROUP + OFFSET, devices)
    top = lax.rem(tile, HBANDS)
    bottom = top + GROUP - 1
    age = lax.div(tile, HBANDS) - block
    near = (
        ((band >= top) & (band <= bottom))
        | ((band == top - 1) & (side == HALF_ROWS - 1))
        | ((band == bottom + 1) & (side == 0))
    )
    own = jnp.where(near & (age == 0), 1.0, 0.0)
    old = jnp.where(near & (age > 0) & (age < 3), 1.0, 0.0)
    before = lax.broadcasted_iota(jnp.int32, (tokens, tokens), 0) < lax.broadcasted_iota(
        jnp.int32, (tokens, tokens), 1
    )
    before = jnp.where(before, 1.0, 0.0).astype(BF16)
    ranks = jnp.dot(
        jnp.concatenate([own, old], 0).astype(BF16), before, preferred_element_type=F32
    )
    rank = jnp.where(
        own > 0.5, ranks[:chips], jnp.where(old > 0.5, slots - 1 - ranks[chips:], -1.0)
    )

    slot = lax.broadcasted_iota(jnp.int32, (rows, tokens), 0).astype(F32)
    low_slot = jnp.where(slot < half, slot, -7.0)
    high_slot = jnp.where(slot < half, slot + half, -7.0)
    blank = jnp.zeros_like(latents)
    codes = jnp.broadcast_to(code, (128, tokens)).astype(BF16)
    low_values = jnp.concatenate([latents, blank, codes], 0)
    high_values = jnp.concatenate([blank, latents, codes], 0)
    low_out = select(
        jnp.concatenate(
            [jnp.where(rank[d : d + 1] == low_slot, 1.0, 0.0).astype(BF16) for d in range(chips)], 0
        ),
        low_values,
    )
    high_out = select(
        jnp.concatenate(
            [jnp.where(rank[d : d + 1] == high_slot, 1.0, 0.0).astype(BF16) for d in range(chips)],
            0,
        ),
        high_values,
    )
    row = lax.broadcasted_iota(jnp.int32, (rows, 128), 0)
    diagonal = row == lax.broadcasted_iota(jnp.int32, (rows, 128), 1)
    for d in range(chips):
        part = slice(d * rows, (d + 1) * rows)
        low_codes = jnp.sum(jnp.where(diagonal, low_out[part, 128:], 0.0), 0, keepdims=True)
        high_codes = jnp.sum(jnp.where(diagonal, high_out[part, 128:], 0.0), 0, keepdims=True)
        body = low_out[part, :128] + high_out[part, :128]
        body = jnp.where(row == rows - 2, low_codes, body)
        body = jnp.where(row == rows - 1, high_codes, body)
        out_ref[part, :] = body.astype(BF16)


def weight_kernel(w_ref, sums_ref):
    first, middle, last = (w_ref[t].astype(F32) * 0.5 for t in range(3))
    outer = first + last
    sums_ref[0] = (outer + middle).astype(BF16)
    sums_ref[1] = (outer - middle).astype(BF16)


def slot_pieces(first, last, half, rows):
    pieces = []
    for high, start, stop in (
        (0, first, min(last, half)),
        (1, max(first, half) - half, last - half),
    ):
        if start < stop:
            pieces.append((high, start // 8 * 8, min(rows, -(-stop // 8) * 8)))
    return pieces


def run(*lists):
    steps = []
    for which, steps_of in enumerate(lists):
        for i, step in enumerate(steps_of):
            steps.append(((i + 0.5) / len(steps_of), which, i, step))
    for step in sorted(steps, key=lambda entry: entry[:3]):
        step[3]()


def main_kernel(
    devices,
    blocks,
    rows,
    half,
    own_slots,
    old_slots,
    slots,
    arrived_ref,
    w_in_ref,
    b_in_ref,
    gain_ref,
    w_mid_hbm,
    w_sum_hbm,
    b_mid_ref,
    out_hbm,
    w_mid_ref,
    spread_ref,
    picked_ref,
    placed_ref,
    edge_ref,
    input_ref,
    active_ref,
    mixed_ref,
    hidden_ref,
    sums_ref,
    mix_ref,
    out_ref,
    w_sem,
    out_sem,
):
    def fetch(k, r):
        source, t = ((w_mid_hbm, 0), (w_sum_hbm, 0), (w_sum_hbm, 1), (w_mid_hbm, 2))[k]
        return pltpu.make_async_copy(source.at[t, r], w_mid_ref.at[k, r], w_sem.at[k, r])

    def start_rows(k):
        def body(r, carry):
            fetch(k, r).start()
            return carry

        lax.fori_loop(0, 3, body, 0)

    def wait_rows(k):
        for r in range(3):
            fetch(k, r).wait()

    for k in (1, 0, 2, 3):
        start_rows(k)
    chips = devices // GROUP
    c_mid = gain_ref.shape[0]
    tile = lax.rem(lax.axis_index("sp") + OFFSET, devices)
    band = lax.rem(tile, HBANDS)
    time_block = lax.div(tile, HBANDS)
    token_rows = HALF_ROWS + 2
    wide = (HB + 2) * HALF_W
    tall = HB * HALF_W

    blank = jnp.zeros((C_LAT, c_mid), BF16)
    for tap in range(3):
        for tap_row in range(4):
            for spot in range(4):
                at = slice(tap_row * PATCH + spot * C_LAT, tap_row * PATCH + (spot + 1) * C_LAT)
                even = w_in_ref[tap, tap_row, spot] if tap_row < 3 and spot < 3 else blank
                odd = w_in_ref[tap, tap_row, spot - 1] if tap_row < 3 and spot > 0 else blank
                spread_ref[tap, at, :c_mid] = even
                spread_ref[tap, at, c_mid:] = odd

    k = lax.broadcasted_iota(jnp.int32, (256, 256), 0)
    lane = lax.broadcasted_iota(jnp.int32, (256, 256), 1)
    within = lane & 63
    swap = ((lane >> 6) ^ (lane >> 7)) & 1
    source = swap * (2 * C_LAT) + jnp.where(
        within < C_LAT,
        within + C_LAT,
        jnp.where(within < 3 * C_LAT, within - C_LAT, within - 3 * C_LAT),
    )
    layout = jnp.where((k == source) | (k == source + 128 + PATCH), 1.0, 0.0).astype(BF16)

    def arrivals(pieces):
        codes, tokens = {}, {}
        for high, start, stop in pieces:
            code_row = rows - 2 + high
            codes[high] = jnp.concatenate(
                [
                    arrived_ref[s * rows + code_row : s * rows + code_row + 1, start:stop]
                    for s in range(chips)
                ],
                1,
            ).astype(F32)
            if stop - start == rows:
                parts = [arrived_ref[...]]
            else:
                parts = [
                    arrived_ref[s * rows + start : s * rows + stop, :]
                    for s in range(chips)
                ]
            tokens[high] = jnp.concatenate(parts, 0)
        return codes, tokens

    by_age = [arrivals(slot_pieces(0, own_slots, half, rows))]
    if blocks > 1:
        by_age.append(arrivals(slot_pieces(slots - old_slots, slots, half, rows)))

    column = lax.broadcasted_iota(jnp.int32, (HALF_W, 1), 0)
    lanes = lax.broadcasted_iota(jnp.int32, (1, 1, 256), 2) & 63
    from_left, from_right = lanes < C_LAT, lanes >= 3 * C_LAT
    upper = lax.broadcasted_iota(jnp.int32, (1, 1, 128), 2) < PATCH

    def picks(f):
        if f < 0:
            return []
        frame = (time_block - (blocks - 1)) * TB + f
        codes, tokens = by_age[0 if f >= TB * (blocks - 1) else 1]

        def pick(start, stop):
            def step():
                picked = {}
                for high in codes:
                    picks = []
                    for i in range(start, stop):
                        token_row = band * HALF_ROWS - 1 + i
                        valid = (
                            (frame >= 0) & (token_row >= 0) & (token_row < HALF_ROWS * HBANDS)
                        )
                        frame_in = lax.max(frame, 0)
                        row_in = lax.max(token_row, 0)
                        base = (
                            lax.rem(lax.div(frame_in, TB), 3) * 3
                            + lax.rem(lax.div(row_in, HALF_ROWS), 3)
                        ) * TILE_TOKENS + (
                            lax.rem(frame_in, TB) * HALF_ROWS + lax.rem(row_in, HALF_ROWS)
                        ) * HALF_W
                        code = jnp.where(valid, place_code(base + column), -1).astype(F32)
                        picks.append(jnp.where(codes[high] == code, 1.0, 0.0).astype(BF16))
                    picked[high] = jnp.dot(
                        jnp.concatenate(picks, 0), tokens[high], preferred_element_type=F32
                    ).astype(BF16)
                    picked_ref[f, start * HALF_W : stop * HALF_W, high * 128 : high * 128 + 128] = (
                        picked[high]
                    )
                for high in range(2):
                    if high not in codes:
                        picked_ref[
                            f, start * HALF_W : stop * HALF_W, high * 128 : high * 128 + 128
                        ] = jnp.zeros(((stop - start) * HALF_W, 128), BF16)

            return step

        return [pick(0, token_rows // 2), pick(token_rows // 2, token_rows)]

    def edges(f):
        if f < 0:
            return []

        def spread():
            placed_ref[f] = jnp.dot(picked_ref[f], layout, preferred_element_type=F32)

        def shift():
            placed = placed_ref[f].reshape(token_rows, HALF_W, 256)
            gap = jnp.zeros((token_rows, 1, 256), F32)
            left = jnp.concatenate([gap, placed[:, :-1]], 1)
            right = jnp.concatenate([placed[:, 1:], gap], 1)
            placed = jnp.where(from_left, left, jnp.where(from_right, right, placed))
            even_rows, odd_rows = placed[:, :, :128], placed[:, :, 128:]
            below = jnp.concatenate([odd_rows[1:], jnp.zeros((1, HALF_W, 128), F32)], 0)
            odd_rows = jnp.where(upper, odd_rows, below)
            for i in range(token_rows):
                start = 2 * i * HALF_W
                edge_ref[f, start : start + HALF_W, :] = even_rows[i].astype(BF16)
                edge_ref[f, start + HALF_W : start + 2 * HALF_W, :] = odd_rows[i].astype(BF16)

        return [spread, shift]

    index = lax.broadcasted_iota(jnp.int32, (HALF_W, 1), 0)
    bias = b_in_ref[...].reshape(1, c_mid)
    gain = gain_ref[...].reshape(1, c_mid)
    bias_mid = b_mid_ref[...].reshape(1, c_mid)

    def convolved(a):
        def convolve(part):
            def step():
                windows, kernels = [], []
                for tap in range(3):
                    f = TB * (blocks - 1) - 4 + a + tap
                    if f < 0:
                        continue
                    windows += [
                        edge_ref[f, 0:wide, :],
                        edge_ref[f, 2 * HALF_W : 2 * HALF_W + wide, :],
                    ]
                    kernels.append(spread_ref[tap, :, part])
                input_ref[a, :, part] = jnp.dot(
                    jnp.concatenate(windows, 1),
                    jnp.concatenate(kernels, 0),
                    preferred_element_type=F32,
                )

            return step

        return [convolve(slice(n, n + 256)) for n in range(0, 2 * c_mid, 256)]

    def activated(a):
        def normalise(r, p):
            def step():
                part = slice(p * c_mid, (p + 1) * c_mid)
                at = slice(r * HALF_W, (r + 1) * HALF_W)
                hidden = (input_ref[a, at, part] + bias).astype(BF16)
                if a >= 2 and 1 <= r <= HB:
                    hidden_ref[a - 2, (r - 1) * HALF_W : r * HALF_W, part] = hidden
                values = hidden.astype(F32)
                mean = jnp.sum(values * values, 1, keepdims=True) * (1.0 / c_mid)
                inverse = lax.rsqrt(mean + 1e-06) * 0.5
                keep = time_block * TB - 2 + a >= 0
                if r in (0, HB + 1):
                    row = band * HB - 1 + r
                    keep = keep & (row >= 0) & (row < HB * HBANDS)
                halved = values * jnp.where(keep, inverse, 0.0) * gain
                active_ref[a, at, part] = (halved + halved * jnp.tanh(halved)).astype(BF16)

            return step

        return [normalise(r, p) for r in range(HB + 2) for p in range(2)]

    halves = 2
    part_rows = tall // halves

    def mix(k):
        def rows_of(start):
            def step():
                at = slice(start, start + 2 * HALF_W)
                one, two, sign = ((0, 2, -1), (1, 2, 1), (2, 1, -1), (1, 3, -1))[k]
                first, second = active_ref[one, at, :], active_ref[two, at, :]
                mixed_ref[k, at, :] = first + second if sign > 0 else first - second

            return step

        return [rows_of(start) for start in range(0, wide, 2 * HALF_W)]

    def product(k, h):
        def piece(source, part, kernel):
            def step():
                windows = [
                    mixed_ref[k, r * HALF_W + h * part_rows : r * HALF_W + (h + 1) * part_rows, source]
                    for r in range(3)
                ]
                value = jnp.dot(
                    jnp.concatenate(windows, 1), kernel(), preferred_element_type=F32
                )
                at = slice(h * part_rows, (h + 1) * part_rows)
                if k == 1:
                    sums_ref[1, at, part] = value
                elif k == 0:
                    sums_ref[0, at, part] = sums_ref[1, at, part] + value
                elif k == 2:
                    sums_ref[0, at, part] = sums_ref[0, at, part] + value
                    sums_ref[1, at, part] = sums_ref[1, at, part] - value
                else:
                    sums_ref[1, at, part] = sums_ref[1, at, part] - value

            return step

        def taps(column_tap, start, stop):
            return [w_mid_ref[k, r, column_tap, :, start:stop] for r in range(3)]

        def straight(start, stop):
            def kernel():
                blocks_of = []
                for r in range(3):
                    for even_tap, odd_tap in ((1, 0), (2, 1)):
                        columns = []
                        if start < c_mid:
                            columns.append(
                                w_mid_ref[k, r, even_tap, :, start : min(stop, c_mid)]
                            )
                        if stop > c_mid:
                            columns.append(
                                w_mid_ref[k, r, odd_tap, :, max(start, c_mid) - c_mid : stop - c_mid]
                            )
                        blocks_of.append(
                            columns[0] if len(columns) == 1 else jnp.concatenate(columns, 1)
                        )
                return jnp.concatenate(blocks_of, 0)

            return kernel

        def side(column_tap, start, stop):
            return lambda: jnp.concatenate(taps(column_tap, start, stop), 0)

        def both_sides(start):
            def kernel():
                width = c_mid - start
                gap = jnp.zeros((c_mid, width), BF16)
                blocks_of = []
                for right, left in zip(taps(2, start, c_mid), taps(0, start, c_mid)):
                    blocks_of.append(jnp.concatenate([right, gap], 1))
                    blocks_of.append(jnp.concatenate([gap, left], 1))
                return jnp.concatenate(blocks_of, 0)

            return kernel

        whole = slice(0, 2 * c_mid)
        straights = [
            piece(whole, slice(n, n + 256), straight(n, n + 256)) for n in range(0, 2 * c_mid, 256)
        ]
        full = c_mid // 256 * 256
        sides = [
            piece(slice(0, c_mid), slice(2 * c_mid, 2 * c_mid + full), side(2, 0, full)),
            piece(
                slice(c_mid, 2 * c_mid), slice(2 * c_mid + full, 2 * c_mid + 2 * full), side(0, 0, full)
            ),
            piece(whole, slice(2 * c_mid + 2 * full, 4 * c_mid), both_sides(full)),
        ]
        return straights[:2] + sides[:2] + straights[2:] + sides[2:]

    full = c_mid // 256 * 256
    rest = c_mid - full

    def finish(o, h):
        out_rows = 2 * part_rows

        def lane_group(g):
            def step():
                at = slice(h * part_rows, (h + 1) * part_rows)
                lanes_of = slice(g * 128, (g + 1) * 128)

                def columns(start):
                    return sums_ref[o, at, start : start + 128]

                if g * 128 < full:
                    right = 2 * c_mid + g * 128
                    left = right + full
                else:
                    right = 2 * c_mid + 2 * full + g * 128 - full
                    left = right + rest
                gap = jnp.zeros((HB // halves, 1, 128), F32)
                shape = (HB // halves, HALF_W, 128)
                to_odd = jnp.concatenate([columns(right).reshape(shape)[:, 1:], gap], 1)
                to_even = jnp.concatenate([gap, columns(left).reshape(shape)[:, :-1]], 1)
                for p, moved in ((0, to_even), (1, to_odd)):
                    start = p * c_mid + g * 128
                    hidden = hidden_ref[o, at, start : start + 128].astype(F32)
                    mix_ref[o, h, g, pl.ds(p, part_rows, stride=2), :] = (
                        columns(start)
                        + moved.reshape(part_rows, 128)
                        + bias_mid[:, lanes_of]
                        + hidden
                    )
                out_ref[o, h * out_rows : (h + 1) * out_rows, lanes_of] = mix_ref[o, h, g].astype(
                    BF16
                )
                leave(o, h, g).start()

            return step

        return [lane_group(g) for g in range(c_mid // 128)]

    def leave(o, h, g):
        out_rows = 2 * part_rows
        lanes_of = pl.ds(g * 128, 128)
        return pltpu.make_async_copy(
            out_ref.at[o, pl.ds(h * out_rows, out_rows), lanes_of],
            out_hbm.at[pl.ds(o * 2 * tall + h * out_rows, out_rows), lanes_of],
            out_sem.at[o, h, g],
        )

    newest = TB * (blocks - 1) - 2
    for f in range(newest):
        run(picks(f) + edges(f))
    run(picks(newest) + picks(newest + 1))
    run(edges(newest), picks(newest + 2))
    run(edges(newest + 1) + convolved(1), picks(newest + 3))
    run(edges(newest + 2) + convolved(2), activated(1))
    run(edges(newest + 3) + convolved(0) + convolved(3), activated(2))
    run(mix(1) + mix(2))
    for k in range(4):
        wait_rows(k)
    run(product(1, 0) + product(1, 1), activated(0) + mix(0))
    run(product(0, 0) + product(0, 1))
    run(product(2, 0) + product(2, 1), activated(3) + mix(3))
    run(product(3, 0), finish(0, 0) + finish(0, 1))
    last = finish(1, 1)
    run(product(3, 1)[:4], finish(1, 0))
    run(last[:1] + product(3, 1)[4:5] + last[1:2] + product(3, 1)[5:] + last[2:])
    for o in range(TB):
        for h in range(halves):
            for g in range(c_mid // 128):
                leave(o, h, g).wait()


def shards(latents, row_cell, w_in, b_in, gain, w_mid, b_mid):
    devices = lax.axis_size("sp")
    tokens = latents.shape[0]
    c_mid = gain.shape[0]
    blocks = min(3, devices // HBANDS)
    chips = devices // GROUP
    pair = tokens // devices
    bands = GROUP + 2
    own_slots = pair * bands + pair
    old_slots = pair * bands * (blocks - 1) + pair
    slots = pair * bands * blocks + pair
    half = -(-slots // 2)
    rows = -(-(half + 2) // 8) * 8
    outgoing = pl.pallas_call(
        functools.partial(pack_kernel, devices, rows, half, slots),
        out_shape=jax.ShapeDtypeStruct((chips * rows, 128), BF16),
        in_specs=[VMEM, VMEM],
        out_specs=VMEM,
        name="pack",
    )(row_cell, latents.T)
    arrived = lax.all_to_all(
        outgoing.reshape(chips, rows, 128), "sp", split_axis=0, concat_axis=0, tiled=True
    )
    w_sum = pl.pallas_call(
        weight_kernel,
        grid=(3, 3),
        out_shape=jax.ShapeDtypeStruct((2, 3, 3, c_mid, c_mid), BF16),
        in_specs=[pl.BlockSpec((3, 1, 1, c_mid, c_mid), lambda i, j: (0, i, j, 0, 0))],
        out_specs=pl.BlockSpec((2, 1, 1, c_mid, c_mid), lambda i, j: (0, i, j, 0, 0)),
        name="weights",
    )(w_mid)
    wide = (HB + 2) * HALF_W
    tall = HB * HALF_W
    frames = TB * blocks
    decoded = pl.pallas_call(
        functools.partial(
            main_kernel, devices, blocks, rows, half, own_slots, old_slots, slots
        ),
        out_shape=jax.ShapeDtypeStruct((TB * HB * W, c_mid), BF16),
        in_specs=[VMEM, VMEM, VMEM, VMEM, HBM, HBM, VMEM],
        out_specs=HBM,
        scratch_shapes=[
            pltpu.VMEM((4, 3, 3, c_mid, c_mid), BF16),
            pltpu.VMEM((3, 4 * PATCH, 2 * c_mid), BF16),
            pltpu.VMEM((frames, (HALF_ROWS + 2) * HALF_W, 256), BF16),
            pltpu.VMEM((frames, (HALF_ROWS + 2) * HALF_W, 256), F32),
            pltpu.VMEM((frames, 2 * (HALF_ROWS + 2) * HALF_W, 128), BF16),
            pltpu.VMEM((TB + 2, wide, 2 * c_mid), F32),
            pltpu.VMEM((TB + 2, wide, 2 * c_mid), BF16),
            pltpu.VMEM((4, wide, 2 * c_mid), BF16),
            pltpu.VMEM((TB, tall, 2 * c_mid), BF16),
            pltpu.VMEM((2, tall, 4 * c_mid), F32),
            pltpu.VMEM((TB, 2, c_mid // 128, tall, 128), F32),
            pltpu.VMEM((TB, 2 * tall, c_mid), BF16),
            pltpu.SemaphoreType.DMA((4, 3)),
            pltpu.SemaphoreType.DMA((TB, 2, c_mid // 128)),
        ],
        compiler_params=pltpu.CompilerParams(vmem_limit_bytes=48 * 1024 * 1024),
        name="block",
    )(
        arrived.reshape(chips * rows, 128),
        w_in,
        b_in,
        gain,
        w_mid,
        pltpu.with_memory_space_constraint(w_sum, pltpu.HBM),
        b_mid,
    )
    return decoded.reshape(1, TB, HB, W, c_mid)


def solution(mesh):
    return jax.shard_map(
        shards,
        mesh=mesh,
        in_specs=(P(("grp", "sp"), None), P(("grp", "sp")), P(), P(), P(), P(), P()),
        out_specs=P(("grp", "sp"), None, None, None, None),
        check_vma=False,
    )
```
